32 devices in a mesh: rows: 8 (over z, y), sub: 4 (over x, core).
Axes of the slice: x: 2, y: 2, z: 4, core: 2. Of those that a mesh axis runs over, the one named last changes fastest.
Arguments:
- snaps_box: bfloat16 [8, 262144], P(None, ('rows', 'sub')), may hold values from -64 to 64
- box_order: int32 [8, 4, 4], P('rows'), may hold values from 0 to 3, as said below
- basis: bfloat16 [262144, 256], P(('rows', 'sub')), may hold values from -20 to 20
Outputs:
- new_modes: bfloat16 [8, 262144], P(None, ('rows', 'sub'))
- coeffs: float32 [8, 256], replicated
- r_factor: float32 [8, 8], replicated
The draws below stay inside these ranges and needn't reach their ends.
Inputs may be any that keep to these rules, and one draw needn't show every extreme that they name: Each box_order[r, t, :] is a permutation of 0 to 3.
All inputs are finite; a program needn't handle non-finite values.
Results may differ from the reference program's by a relative error of at most 0.001.
The reference program's roundings to bfloat16 on the way (of `snapshots` and `rounded`) count: a program that leaves them out, or rounds other values in their place, can miss the bound.
Values may be sent and summed in bfloat16 or wider, within the bound.
No kernel may reach another device: no remote copies, remote signals or barrier semaphores. Data moves between devices by JAX's collectives and lax.ppermute only.
A program may use at most 64 MiB of HBM per device.

```python
import jax
import jax.numpy as jnp
from jax import lax

SNAPS = 8
RANK = 256
BLOCK = 2048
CELLS = 262144
N_ROWS = 8
N_SUB = 4


def snapshot_rows(key):
    return 10.5 * jax.random.truncated_normal(jax.random.fold_in(key, 11), -5.5, 5.5, (SNAPS, CELLS), jnp.float32)


def permute_one(subkey):
    return jax.random.permutation(subkey, N_SUB)


def order_table(key):
    key_list = jax.random.split(jax.random.fold_in(key, 7), N_ROWS * N_SUB)
    return jax.vmap(permute_one)(key_list).reshape(N_ROWS, N_SUB, N_SUB).astype(jnp.int32)


def draw_box_order(key, part):
    return order_table(key)


def draw_snaps_box(key, part):
    values = snapshot_rows(key)
    order = order_table(key)
    layered = values.reshape(SNAPS, N_ROWS, N_SUB, N_SUB, BLOCK)
    picked = jnp.take_along_axis(layered, order[None, :, :, :, None], axis=3)
    box_layout = jnp.transpose(picked, (0, 1, 3, 2, 4))
    return box_layout.reshape(SNAPS, CELLS).astype(jnp.bfloat16)


def draw_basis(key, part):
    values = snapshot_rows(key)
    mixing = jax.random.truncated_normal(jax.random.fold_in(key, 13), -5.0, 5.0, (SNAPS, RANK), jnp.float32) * (0.08 / math_sqrt(RANK))
    noise_part = jax.random.truncated_normal(jax.random.fold_in(key, 17), -5.5, 5.5, (CELLS, RANK), jnp.float32)
    joined = noise_part + jnp.dot(values.T, mixing, precision=lax.Precision.HIGHEST)
    return joined.astype(jnp.bfloat16)


def math_sqrt(number):
    return float(number) ** 0.5


def setup_inputs(seed: int = 0) -> dict:
    seeds = jax.random.split(jax.random.key(seed), 4)
    return {
        "snaps_box": draw_snaps_box(jax.random.fold_in(seeds[3], 71), 0),
        "box_order": draw_box_order(jax.random.fold_in(seeds[3], 71), 0),
        "basis": draw_basis(jax.random.fold_in(seeds[3], 71), 0),
    }


def reference(snaps_box, box_order, basis):
    snapcount = snaps_box.shape[0]
    cell_total = snaps_box.shape[1]
    block_len = cell_total // (N_ROWS * N_SUB * N_SUB)
    boxes = snaps_box.astype(jnp.float32).reshape(snapcount, N_ROWS, N_SUB, N_SUB, block_len)
    placing = (box_order[..., None] == jnp.arange(N_SUB, dtype=jnp.int32)).astype(jnp.float32)
    row_data = jnp.einsum('rtsp,arstb->artpb', placing, boxes)
    snapshots = row_data.reshape(snapcount, cell_total).astype(jnp.bfloat16)
    raw_sums = jnp.dot(snapshots.astype(jnp.float32), basis.astype(jnp.float32), preferred_element_type=jnp.float32)
    coeffs = raw_sums / cell_total
    rounded = coeffs.astype(jnp.bfloat16)
    fitted = lax.dot_general(rounded.astype(jnp.float32), basis.astype(jnp.float32), (((1,), (1,)), ((), ())), preferred_element_type=jnp.float32)
    residual = snapshots.astype(jnp.float32) - fitted
    wgram = jnp.dot(residual, residual.T, precision=lax.Precision.HIGHEST) / cell_total
    lower_tri = jnp.linalg.cholesky(wgram)
    modes = jax.scipy.linalg.solve_triangular(lower_tri, residual, lower=True)
    return (modes.astype(jnp.bfloat16), coeffs, lower_tri.T)
```

```python
import jax
import jax.numpy as jnp
from jax import lax
from jax.experimental import pallas as pl
from jax.experimental.pallas import tpu as pltpu
from jax.sharding import PartitionSpec as P

AXES = ("rows", "sub")
HIGH = lax.Precision.HIGHEST
LANES = 128
GUARD = 1.0 / 64.0
VMEM = pl.BlockSpec(memory_space=pltpu.VMEM)
SMEM = pl.BlockSpec(memory_space=pltpu.SMEM)
F32 = jnp.float32
MB = 1 << 20


def nt(a, b, precision=None):
    return lax.dot_general(
        a, b, (((1,), (1,)), ((), ())), precision=precision, preferred_element_type=F32
    )


def lane_at_least(shape, bound):
    return lax.broadcasted_iota(jnp.int32, shape, len(shape) - 1) >= bound


def gram_kernel(basis_ref, fold_ref):
    rank = basis_ref.shape[1]
    half, quarter = rank // 2, rank // 4
    total = lax.dot_general(
        basis_ref[...], basis_ref[...], (((0,), (0,)), ((), ())), preferred_element_type=F32
    )
    upper = lane_at_least((quarter, half), quarter)
    fold_ref[0:quarter] = jnp.where(upper, 2.0, 1.0) * total[0:quarter, 0:half]
    fold_ref[quarter : 2 * quarter] = jnp.where(
        upper, total[quarter:half, 0:half], total[half : 3 * quarter, half:]
    )
    fold_ref[2 * quarter : 3 * quarter] = jnp.where(upper, 1.0, 2.0) * total[3 * quarter :, half:]
    fold_ref[3 * quarter : 3 * quarter + half] = 2.0 * total[0:half, half:]


def project_kernel(order_ref, snaps_ref, basis_ref, fold_ref, out_ref):
    groups, snapcount, block_len = snaps_ref.shape
    fold_rows = fold_ref.shape[0]
    rank = basis_ref.shape[1]
    raw = jnp.zeros((snapcount, rank), F32)
    own = jnp.zeros((snapcount, snapcount), F32)
    for source in range(groups):
        start = pl.multiple_of(order_ref[source] * block_len, block_len)
        block = snaps_ref[source]
        raw += jnp.dot(block, basis_ref[pl.ds(start, block_len), :], preferred_element_type=F32)
        own += nt(block, block)
    out_ref[0:fold_rows] = fold_ref[...]
    at = fold_rows
    for part in range(rank // LANES):
        out_ref[at : at + snapcount] = raw[:, part * LANES : (part + 1) * LANES]
        at += snapcount
    out_ref[at:] = jnp.zeros((out_ref.shape[0] - at, LANES), F32)
    out_ref[at : at + snapcount, 0:snapcount] = own


def column(matrix, index):
    return matrix[:, index : index + 1]


def factor(gram, scale):
    count = gram.shape[0]
    row_id = lax.broadcasted_iota(jnp.int32, (count, count), 0)
    col_id = lax.broadcasted_iota(jnp.int32, (count, count), 1)
    eye = (row_id == col_id).astype(F32)
    both = jnp.concatenate([gram, eye], axis=1)
    rows = lax.broadcasted_iota(jnp.int32, both.shape, 0)
    for step in range(count - 1):
        factors = column(both, step)
        ratio = factors / factors[step : step + 1]
        both -= jnp.where(rows > step, ratio * both[step : step + 1], 0.0)
    pivots = jnp.sum(both[:, 0:count] * eye, axis=1, keepdims=True)
    weak = jnp.sum(jnp.where(pivots >= GUARD * scale, 0.0, 1.0))
    both = both / jnp.sqrt(pivots)
    return jnp.where(row_id <= col_id, both[:, 0:count], 0.0), both[:, count:], weak


def finish_kernel(
    cell_total,
    order_ref,
    side_ref,
    mine_ref,
    other_ref,
    snaps_ref,
    basis_ref,
    modes_ref,
    coeffs_ref,
    upper_ref,
    weak_ref,
    sums_ref,
    resid_ref,
):
    groups, snapcount, block_len = snaps_ref.shape
    rank = basis_ref.shape[1]
    half, quarter = rank // 2, rank // 4
    share = mine_ref.shape[0]
    first = side_ref[0] == 0
    sums_ref[0:share] = jnp.where(first, mine_ref[...], other_ref[...])
    sums_ref[share:] = jnp.where(first, other_ref[...], mine_ref[...])
    fold_rows = 3 * quarter + half
    parts = rank // LANES
    raw = jnp.concatenate(
        [sums_ref[fold_rows + k * snapcount : fold_rows + (k + 1) * snapcount] for k in range(parts)],
        axis=1,
    )
    at = fold_rows + parts * snapcount
    own = sums_ref[at : at + snapcount, 0:snapcount]
    coeffs = raw / cell_total
    coeffs_ref[...] = coeffs
    narrow = coeffs.astype(jnp.bfloat16)
    rounded = narrow.astype(F32)

    for source in range(groups):
        start = pl.multiple_of(order_ref[source] * block_len, block_len)
        fitted = nt(narrow, basis_ref[pl.ds(start, block_len), :])
        resid_ref[source] = snaps_ref[source].astype(F32) - fitted

    upper = lane_at_least((quarter, half), quarter)
    middle = sums_ref[quarter : 2 * quarter]
    left = jnp.concatenate([sums_ref[0:quarter], jnp.where(upper, middle, 0.0)], axis=0)
    right = jnp.concatenate(
        [
            sums_ref[3 * quarter : fold_rows],
            jnp.where(upper, 0.0, middle),
            sums_ref[2 * quarter : 3 * quarter],
        ],
        axis=0,
    )
    spread = jnp.concatenate(
        [
            jnp.dot(rounded[:, 0:half], left, precision=HIGH, preferred_element_type=F32),
            jnp.dot(rounded, right, precision=HIGH, preferred_element_type=F32),
        ],
        axis=1,
    )
    cross = nt(raw, rounded, HIGH)
    quad = nt(spread, rounded, HIGH)
    gram = (own - (cross + cross.T) + 0.5 * (quad + quad.T)) / cell_total
    size = own + 2.0 * jnp.abs(cross) + jnp.abs(quad)
    eye = lax.broadcasted_iota(jnp.int32, size.shape, 0) == lax.broadcasted_iota(
        jnp.int32, size.shape, 1
    )
    scale = jnp.sum(jnp.where(eye, size, 0.0), axis=1, keepdims=True) / cell_total
    upper_factor, inverse, weak = factor(gram, scale)
    upper_ref[...] = upper_factor
    weak_ref[0] = weak

    for source in range(groups):
        start = pl.multiple_of(order_ref[source] * block_len, block_len)
        modes = column(inverse, 0) * resid_ref[source, 0:1, :]
        for row in range(1, snapcount):
            modes += column(inverse, row) * resid_ref[source, row : row + 1, :]
        modes_ref[:, pl.ds(start, block_len)] = modes.astype(jnp.bfloat16)


def exchange(value, total, masks):
    def partner(index):
        return index ^ masks[bin(index).count("1") % 2]

    return lax.ppermute(value, AXES, [(index, partner(index)) for index in range(total)])


def all_sum(value, total):
    value = value + exchange(value, total, (1, 1))
    for bit in range(1, total.bit_length() - 1):
        mask = (1 << bit) | 1
        value = value + exchange(value, total, (mask, mask))
    return value


def local(snaps_box, box_order, basis):
    snapcount = snaps_box.shape[0]
    local_cells, rank = basis.shape
    groups = lax.axis_size("sub")
    total = lax.axis_size("rows") * groups
    block_len = local_cells // groups
    cell_total = local_cells * total
    position = lax.axis_index("sub")
    order_row = lax.dynamic_index_in_dim(box_order[0], position, 0, keepdims=False)
    device = lax.axis_index("rows") * groups + position
    side = lax.population_count(device) % 2

    blocks = snaps_box.reshape(snapcount, groups, block_len).transpose(1, 0, 2)
    received = lax.all_to_all(blocks, "sub", split_axis=0, concat_axis=0, tiled=True)

    half, quarter = rank // 2, rank // 4
    fold_rows = 3 * quarter + half
    fold = pl.pallas_call(
        gram_kernel,
        out_shape=jax.ShapeDtypeStruct((fold_rows, half), F32),
        in_specs=[VMEM],
        out_specs=VMEM,
        compiler_params=pltpu.CompilerParams(vmem_limit_bytes=24 * MB),
        cost_estimate=pl.CostEstimate(
            flops=2 * local_cells * rank * rank,
            bytes_accessed=2 * local_cells * rank,
            transcendentals=0,
        ),
    )(basis)
    used = fold_rows + (rank // LANES + 1) * snapcount
    share = -(-used // 16) * 8
    packed = pl.pallas_call(
        project_kernel,
        out_shape=jax.ShapeDtypeStruct((2 * share, LANES), F32),
        in_specs=[SMEM, VMEM, VMEM, VMEM],
        out_specs=VMEM,
        compiler_params=pltpu.CompilerParams(vmem_limit_bytes=24 * MB),
    )(order_row, received, basis, fold)

    packed = packed + exchange(packed, total, (1, 1))
    mine = lax.dynamic_slice_in_dim(packed, side * share, share, 0)
    masks = [(1 << bit) | 1 for bit in range(1, total.bit_length() - 1)]
    swapped = list(masks)
    for index in range(0, len(masks) - 1, 2):
        swapped[index], swapped[index + 1] = masks[index + 1], masks[index]
    for pair in zip(masks, swapped):
        mine = mine + exchange(mine, total, pair)
    other = exchange(mine, total, (1, 1))

    modes, coeffs, r_factor, weak = pl.pallas_call(
        lambda *refs: finish_kernel(cell_total, *refs),
        out_shape=(
            jax.ShapeDtypeStruct((snapcount, local_cells), jnp.bfloat16),
            jax.ShapeDtypeStruct((snapcount, rank), F32),
            jax.ShapeDtypeStruct((snapcount, snapcount), F32),
            jax.ShapeDtypeStruct((1,), F32),
        ),
        in_specs=[SMEM, SMEM, VMEM, VMEM, VMEM, VMEM],
        out_specs=(VMEM, VMEM, VMEM, SMEM),
        scratch_shapes=[
            pltpu.VMEM((2 * share, LANES), F32),
            pltpu.VMEM((groups, snapcount, block_len), F32),
        ],
        compiler_params=pltpu.CompilerParams(vmem_limit_bytes=24 * MB),
    )(order_row, side.reshape(1), mine, other, received, basis)

    def direct(_):
        ordered = jnp.argsort(order_row)
        snapshots = jnp.take(received, ordered, axis=0).transpose(1, 0, 2)
        snapshots = snapshots.reshape(snapcount, local_cells).astype(F32)
        residual = snapshots - nt(coeffs.astype(jnp.bfloat16), basis)
        wgram = all_sum(jnp.dot(residual, residual.T, precision=HIGH) / cell_total, total)
        lower = jnp.linalg.cholesky(wgram)
        solved = jax.scipy.linalg.solve_triangular(lower, residual, lower=True)
        return solved.astype(jnp.bfloat16), lower.T

    modes, r_factor = lax.cond(weak[0] > 0.0, direct, lambda ready: ready, (modes, r_factor))
    return modes, coeffs, r_factor


def solution(mesh):
    return jax.shard_map(
        local,
        mesh=mesh,
        in_specs=(P(None, AXES), P("rows", None, None), P(AXES, None)),
        out_specs=(P(None, AXES), P(), P()),
        check_vma=False,
    )
```

```python
import jax
import jax.numpy as jnp
from jax import lax
from jax.experimental import pallas as pl
from jax.experimental.pallas import tpu as pltpu
from jax.sharding import PartitionSpec as P

AXES = ("rows", "sub")
HIGH = lax.Precision.HIGHEST
LANES = 128
GUARD = 1.0 / 64.0
CHUNKS = 8
LIMIT = 16 * 1048576
VMEM = pl.BlockSpec(memory_space=pltpu.VMEM)
SMEM = pl.BlockSpec(memory_space=pltpu.SMEM)
F32 = jnp.float32


def nt(a, b, precision=None):
    return lax.dot_general(
        a, b, (((1,), (1,)), ((), ())), precision=precision, preferred_element_type=F32
    )


def lane_at_least(shape, bound):
    return lax.broadcasted_iota(jnp.int32, shape, len(shape) - 1) >= bound


def gram_kernel(basis_ref, fold_ref, near_ref, sems):
    cells, rank = near_ref.shape
    half, quarter = rank // 2, rank // 4
    chunk = cells // CHUNKS

    def load(index):
        part = pl.ds(index * chunk, chunk)
        return pltpu.make_async_copy(basis_ref.at[part], near_ref.at[part], sems.at[index])

    for index in range(CHUNKS):
        load(index).start()
    total = jnp.zeros((rank, rank), F32)
    for index in range(CHUNKS):
        load(index).wait()
        part = near_ref[index * chunk : (index + 1) * chunk]
        total += lax.dot_general(
            part, part, (((0,), (0,)), ((), ())), preferred_element_type=F32
        )
    upper = lane_at_least((quarter, half), quarter)
    fold_ref[0:quarter] = jnp.where(upper, 2.0, 1.0) * total[0:quarter, 0:half]
    fold_ref[quarter : 2 * quarter] = jnp.where(
        upper, total[quarter:half, 0:half], total[half : 3 * quarter, half:]
    )
    fold_ref[2 * quarter : 3 * quarter] = jnp.where(upper, 1.0, 2.0) * total[3 * quarter :, half:]
    fold_ref[3 * quarter : 3 * quarter + half] = 2.0 * total[0:half, half:]


def device_index():
    return lax.axis_index("rows") * lax.axis_size("sub") + lax.axis_index("sub")


def parity(device, total):
    value = device
    for bit in range(1, (total - 1).bit_length()):
        value = value ^ (device >> bit)
    return value & 1


def fetch_kernel(far_ref, near_ref, sem):
    copy = pltpu.make_async_copy(far_ref, near_ref, sem)
    copy.start()
    copy.wait()


def pack_kernel(kept, own_ref, peer_ref, keep_ref, send_ref):
    position = lax.axis_index("sub")
    half = len(kept) // 2
    for source, ref in enumerate((own_ref, peer_ref)):
        for index, offset in enumerate(kept):
            out = keep_ref if index < half else send_ref
            out[source, index % half] = ref[position ^ offset]


def starts(order_ref, sources, block_len):
    position = lax.axis_index("sub")
    return [
        pl.multiple_of(order_ref[0, position, position ^ source] * block_len, block_len)
        for source in sources
    ]


def project_kernel(sources, total, order_ref, keep_ref, far_ref, basis_ref, fold_ref, mine_ref, send_ref, out_ref):
    near, snapcount, block_len = keep_ref.shape
    share = mine_ref.shape[0]
    fold_rows = fold_ref.shape[0]
    rank = basis_ref.shape[1]
    raw = jnp.zeros((snapcount, rank), F32)
    own = jnp.zeros((snapcount, snapcount), F32)
    for index, start in enumerate(starts(order_ref, sources, block_len)):
        block = keep_ref[index] if index < near else far_ref[index - near]
        raw += jnp.dot(block, basis_ref[pl.ds(start, block_len), :], preferred_element_type=F32)
        own += nt(block, block)
    out_ref[0:fold_rows] = fold_ref[...]
    at = fold_rows
    for part in range(rank // LANES):
        out_ref[at : at + snapcount] = raw[:, part * LANES : (part + 1) * LANES]
        at += snapcount
    out_ref[at:] = jnp.zeros((out_ref.shape[0] - at, LANES), F32)
    out_ref[at : at + snapcount, 0:snapcount] = own
    side = parity(device_index(), total)
    mine_ref[...] = out_ref[pl.ds(pl.multiple_of(side * share, 8), share)]
    send_ref[...] = out_ref[pl.ds(pl.multiple_of((1 - side) * share, 8), share)]


def column(matrix, index):
    return matrix[:, index : index + 1]


def factor(gram, scale):
    count = gram.shape[0]
    row_id = lax.broadcasted_iota(jnp.int32, (count, count), 0)
    col_id = lax.broadcasted_iota(jnp.int32, (count, count), 1)
    eye = (row_id == col_id).astype(F32)
    both = jnp.concatenate([gram, eye], axis=1)
    rows = lax.broadcasted_iota(jnp.int32, both.shape, 0)
    for step in range(count - 1):
        factors = column(both, step)
        ratio = factors / factors[step : step + 1]
        both -= jnp.where(rows > step, ratio * both[step : step + 1], 0.0)
    pivots = jnp.sum(both[:, 0:count] * eye, axis=1, keepdims=True)
    weak = jnp.sum(jnp.where(pivots >= GUARD * scale, 0.0, 1.0))
    both = both / jnp.sqrt(pivots)
    return jnp.where(row_id <= col_id, both[:, 0:count], 0.0), both[:, count:], weak


def finish_kernel(
    sources,
    total,
    order_ref,
    mine_ref,
    other_ref,
    keep_ref,
    far_ref,
    basis_ref,
    modes_ref,
    coeffs_ref,
    upper_ref,
    weak_ref,
    sums_ref,
    resid_ref,
):
    near, snapcount, block_len = keep_ref.shape
    cells, rank = basis_ref.shape
    cell_total = cells * total
    half, quarter = rank // 2, rank // 4
    share = mine_ref.shape[0]
    first = parity(device_index(), total) == 0
    places = starts(order_ref, sources, block_len)
    sums_ref[0:share] = jnp.where(first, mine_ref[...], other_ref[...])
    sums_ref[share:] = jnp.where(first, other_ref[...], mine_ref[...])
    fold_rows = 3 * quarter + half
    parts = rank // LANES
    raw = jnp.concatenate(
        [sums_ref[fold_rows + k * snapcount : fold_rows + (k + 1) * snapcount] for k in range(parts)],
        axis=1,
    )
    at = fold_rows + parts * snapcount
    own = sums_ref[at : at + snapcount, 0:snapcount]
    coeffs = raw / cell_total
    coeffs_ref[...] = coeffs
    narrow = coeffs.astype(jnp.bfloat16)
    rounded = narrow.astype(F32)

    for index, start in enumerate(places):
        fitted = nt(narrow, basis_ref[pl.ds(start, block_len), :])
        block = keep_ref[index] if index < near else far_ref[index - near]
        resid_ref[index] = block.astype(F32) - fitted

    upper = lane_at_least((quarter, half), quarter)
    middle = sums_ref[quarter : 2 * quarter]
    left = jnp.concatenate([sums_ref[0:quarter], jnp.where(upper, middle, 0.0)], axis=0)
    right = jnp.concatenate(
        [
            sums_ref[3 * quarter : fold_rows],
            jnp.where(upper, 0.0, middle),
            sums_ref[2 * quarter : 3 * quarter],
        ],
        axis=0,
    )
    spread = jnp.concatenate(
        [
            jnp.dot(rounded[:, 0:half], left, precision=HIGH, preferred_element_type=F32),
            jnp.dot(rounded, right, precision=HIGH, preferred_element_type=F32),
        ],
        axis=1,
    )
    cross = nt(raw, rounded, HIGH)
    quad = nt(spread, rounded, HIGH)
    gram = (own - (cross + cross.T) + 0.5 * (quad + quad.T)) / cell_total
    size = own + 2.0 * jnp.abs(cross) + jnp.abs(quad)
    eye = lax.broadcasted_iota(jnp.int32, size.shape, 0) == lax.broadcasted_iota(
        jnp.int32, size.shape, 1
    )
    scale = jnp.sum(jnp.where(eye, size, 0.0), axis=1, keepdims=True) / cell_total
    upper_factor, inverse, weak = factor(gram, scale)
    upper_ref[...] = upper_factor
    weak_ref[0] = weak

    for index, start in enumerate(places):
        modes = column(inverse, 0) * resid_ref[index, 0:1, :]
        for row in range(1, snapcount):
            modes += column(inverse, row) * resid_ref[index, row : row + 1, :]
        modes_ref[:, pl.ds(start, block_len)] = modes.astype(jnp.bfloat16)


def exchange(value, total, masks):
    def partner(index):
        return index ^ masks[bin(index).count("1") % 2]

    return lax.ppermute(value, AXES, [(index, partner(index)) for index in range(total)])


def flips(count):
    return [(1 << bit) | 1 for bit in range(1, count.bit_length() - 1)]


def all_sum(value, total):
    for mask in [1] + flips(total):
        value = value + exchange(value, total, (mask, mask))
    return value


def kernel_call(kernel, outputs, in_specs, out_specs, scratch=(), **options):
    return pl.pallas_call(
        kernel,
        out_shape=outputs,
        in_specs=in_specs,
        out_specs=out_specs,
        scratch_shapes=scratch,
        compiler_params=pltpu.CompilerParams(vmem_limit_bytes=LIMIT),
        **options,
    )


def spread_boxes(boxes, groups, total):
    like = jax.ShapeDtypeStruct
    peer = exchange(boxes, total, (1, 1))
    own = kernel_call(
        fetch_kernel,
        like(boxes.shape, boxes.dtype),
        [pl.BlockSpec(memory_space=pltpu.HBM)],
        VMEM,
        [pltpu.SemaphoreType.DMA(())],
        cost_estimate=pl.CostEstimate(
            flops=0, bytes_accessed=2 * boxes.size, transcendentals=0
        ),
    )(boxes)
    kept, sources = [0], [0, 1]
    for mask in flips(groups):
        kept = kept + [offset ^ mask for offset in kept]
    half = len(kept) // 2
    shape = like((2, half) + boxes.shape[1:], boxes.dtype)
    keep, send = kernel_call(
        lambda *refs: pack_kernel(kept, *refs), (shape, shape), [VMEM, VMEM], (VMEM, VMEM)
    )(own, peer)
    for mask in reversed(flips(groups)):
        far = exchange(send, total, (mask, mask))
        sources = sources + [source ^ mask for source in sources]
        if half == 1:
            return keep[:, 0], far[:, 0], sources
        both = jnp.concatenate([keep, far], axis=0)
        half //= 2
        keep, send = both[:, :half], both[:, half:]


def local(snaps_box, box_order, basis):
    like = jax.ShapeDtypeStruct
    snapcount = snaps_box.shape[0]
    local_cells, rank = basis.shape
    groups = lax.axis_size("sub")
    total = lax.axis_size("rows") * groups
    block_len = local_cells // groups
    cell_total = local_cells * total

    boxes = snaps_box.reshape(snapcount, groups, block_len).transpose(1, 0, 2)
    keep, far, sources = spread_boxes(boxes, groups, total)

    half, quarter = rank // 2, rank // 4
    fold_rows = 3 * quarter + half
    fold, near = kernel_call(
        gram_kernel,
        (like((fold_rows, half), F32), like(basis.shape, basis.dtype)),
        [pl.BlockSpec(memory_space=pltpu.HBM)],
        (VMEM, VMEM),
        [pltpu.SemaphoreType.DMA((CHUNKS,))],
        cost_estimate=pl.CostEstimate(
            flops=2 * local_cells * rank * rank,
            bytes_accessed=2 * local_cells * rank,
            transcendentals=0,
        ),
    )(basis)
    used = fold_rows + (rank // LANES + 1) * snapcount
    share = -(-used // 16) * 8
    part = like((share, LANES), F32)
    mine, send = kernel_call(
        lambda *refs: project_kernel(sources, total, *refs),
        (part, part),
        [SMEM, VMEM, VMEM, VMEM, VMEM],
        (VMEM, VMEM),
        [pltpu.VMEM((2 * share, LANES), F32)],
    )(box_order, keep, far, near, fold)

    mine = mine + exchange(send, total, (1, 1))
    masks = flips(total)
    swapped = list(masks)
    for index in range(0, len(masks) - 1, 2):
        swapped[index], swapped[index + 1] = masks[index + 1], masks[index]
    for pair in zip(masks, swapped):
        mine = mine + exchange(mine, total, pair)
    other = exchange(mine, total, (1, 1))

    modes, coeffs, r_factor, weak = kernel_call(
        lambda *refs: finish_kernel(sources, total, *refs),
        (
            like((snapcount, local_cells), jnp.bfloat16),
            like((snapcount, rank), F32),
            like((snapcount, snapcount), F32),
            like((1,), F32),
        ),
        [SMEM, VMEM, VMEM, VMEM, VMEM, VMEM],
        (VMEM, VMEM, VMEM, SMEM),
        [
            pltpu.VMEM((2 * share, LANES), F32),
            pltpu.VMEM((groups, snapcount, block_len), F32),
        ],
    )(box_order, mine, other, keep, far, near)

    def direct(_):
        position = lax.axis_index("sub")
        order_row = lax.dynamic_index_in_dim(box_order[0], position, 0, keepdims=False)
        held = position ^ jnp.array(sources, dtype=jnp.int32)
        ordered = jnp.argsort(order_row[held])
        snapshots = jnp.take(jnp.concatenate([keep, far]), ordered, axis=0).transpose(1, 0, 2)
        snapshots = snapshots.reshape(snapcount, local_cells).astype(F32)
        residual = snapshots - nt(coeffs.astype(jnp.bfloat16), basis)
        wgram = all_sum(jnp.dot(residual, residual.T, precision=HIGH) / cell_total, total)
        lower = jnp.linalg.cholesky(wgram)
        solved = jax.scipy.linalg.solve_triangular(lower, residual, lower=True)
        return solved.astype(jnp.bfloat16), lower.T

    modes, r_factor = lax.cond(weak[0] > 0.0, direct, lambda ready: ready, (modes, r_factor))
    return modes, coeffs, r_factor


def solution(mesh):
    return jax.shard_map(
        local,
        mesh=mesh,
        in_specs=(P(None, AXES), P("rows", None, None), P(AXES, None)),
        out_specs=(P(None, AXES), P(), P()),
        check_vma=False,
    )
```

```python
import jax
import jax.numpy as jnp
from jax import lax
from jax.experimental import pallas as pl
from jax.experimental.pallas import tpu as pltpu
from jax.sharding import PartitionSpec as P

AXES = ("rows", "sub")
HIGH = lax.Precision.HIGHEST
LANES = 128
GUARD = 1.0 / 64.0
STRETCHES = 8
HBM = pl.BlockSpec(memory_space=pltpu.HBM)
ANY = pl.BlockSpec(memory_space=pl.ANY)
DMA = pltpu.SemaphoreType.DMA
LIMIT = 16 * 1048576
VMEM = pl.BlockSpec(memory_space=pltpu.VMEM)
SMEM = pl.BlockSpec(memory_space=pltpu.SMEM)
F32 = jnp.float32


def nt(a, b, precision=None):
    return lax.dot_general(
        a, b, (((1,), (1,)), ((), ())), precision=precision, preferred_element_type=F32
    )


def lane_at_least(shape, bound):
    return lax.broadcasted_iota(jnp.int32, shape, len(shape) - 1) >= bound


def gram_of(part):
    return lax.dot_general(part, part, (((0,), (0,)), ((), ())), preferred_element_type=F32)


def copies(source_ref, target_ref, bounds, sems):
    made = []
    for index, (low, high) in enumerate(bounds):
        part = pl.ds(low, high - low)
        made.append(
            pltpu.make_async_copy(source_ref.at[part], target_ref.at[part], sems.at[index])
        )
        made[index].start()
    return made


def open_kernel(done, boxes_ref, basis_ref, own_ref, near_ref, total_ref, box_sem, sems):
    box = pltpu.make_async_copy(boxes_ref, own_ref, box_sem)
    box.start()
    (rows,) = copies(basis_ref, near_ref, [(0, done)], sems)
    rows.wait()
    total_ref[...] = gram_of(near_ref[0:done])
    box.wait()


def gram_kernel(bounds, basis_ref, held_ref, total_ref, fold_ref, near_ref, sems):
    rank = near_ref.shape[1]
    half, quarter = rank // 2, rank // 4
    total = total_ref[...]
    for copy, (low, high) in zip(copies(basis_ref, near_ref, bounds, sems), bounds):
        copy.wait()
        total += gram_of(near_ref[low:high])
    upper = lane_at_least((quarter, half), quarter)
    fold_ref[0:quarter] = jnp.where(upper, 2.0, 1.0) * total[0:quarter, 0:half]
    fold_ref[quarter : 2 * quarter] = jnp.where(
        upper, total[quarter:half, 0:half], total[half : 3 * quarter, half:]
    )
    fold_ref[2 * quarter : 3 * quarter] = jnp.where(upper, 1.0, 2.0) * total[3 * quarter :, half:]
    fold_ref[3 * quarter : 3 * quarter + half] = 2.0 * total[0:half, half:]


def device_index():
    return lax.axis_index("rows") * lax.axis_size("sub") + lax.axis_index("sub")


def parity(device, total):
    value = device
    for bit in range(1, (total - 1).bit_length()):
        value = value ^ (device >> bit)
    return value & 1


def pack_kernel(kept, own_ref, peer_ref, keep_ref, send_ref):
    position = lax.axis_index("sub")
    half = len(kept) // 2
    for source, ref in enumerate((own_ref, peer_ref)):
        for index, offset in enumerate(kept):
            out = keep_ref if index < half else send_ref
            out[source, index % half] = ref[position ^ offset]


def project_kernel(
    sources,
    total,
    order_hbm,
    keep_ref,
    far_ref,
    basis_ref,
    fold_ref,
    mine_ref,
    send_ref,
    placed_ref,
    out_ref,
    order_ref,
    sem,
):
    table = pltpu.make_async_copy(order_hbm, order_ref, sem)
    table.start()
    near, snapcount, block_len = keep_ref.shape
    share = mine_ref.shape[0]
    fold_rows = fold_ref.shape[0]
    rank = basis_ref.shape[1]
    blocks = [keep_ref[index] for index in range(near)]
    blocks += [far_ref[index] for index in range(len(sources) - near)]
    out_ref[0:fold_rows] = fold_ref[...]
    own = nt(blocks[0], blocks[0])
    for block in blocks[1:]:
        own += nt(block, block)
    table.wait()
    position = lax.axis_index("sub")
    raw = jnp.zeros((snapcount, rank), F32)
    for source, block in zip(sources, blocks):
        start = order_ref[0, position, position ^ source] * block_len
        start = pl.multiple_of(start, block_len)
        raw += jnp.dot(block, basis_ref[pl.ds(start, block_len), :], preferred_element_type=F32)
        placed_ref[:, pl.ds(start, block_len)] = block
    at = fold_rows
    for part in range(rank // LANES):
        out_ref[at : at + snapcount] = raw[:, part * LANES : (part + 1) * LANES]
        at += snapcount
    out_ref[at:] = jnp.zeros((out_ref.shape[0] - at, LANES), F32)
    out_ref[at : at + snapcount, 0:snapcount] = own
    side = parity(device_index(), total)
    mine_ref[...] = out_ref[pl.ds(pl.multiple_of(side * share, 8), share)]
    send_ref[...] = out_ref[pl.ds(pl.multiple_of((1 - side) * share, 8), share)]


def column(matrix, index):
    return matrix[:, index : index + 1]


def factor(gram, scale):
    count = gram.shape[0]
    row_id = lax.broadcasted_iota(jnp.int32, (count, count), 0)
    col_id = lax.broadcasted_iota(jnp.int32, (count, count), 1)
    eye = (row_id == col_id).astype(F32)
    both = jnp.concatenate([gram, eye], axis=1)
    rows = lax.broadcasted_iota(jnp.int32, both.shape, 0)
    for step in range(count - 1):
        factors = column(both, step)
        ratio = factors / factors[step : step + 1]
        both -= jnp.where(rows > step, ratio * both[step : step + 1], 0.0)
    pivots = jnp.sum(both[:, 0:count] * eye, axis=1, keepdims=True)
    weak = jnp.sum(jnp.where(pivots >= GUARD * scale, 0.0, 1.0))
    both = both / jnp.sqrt(pivots)
    return jnp.where(row_id <= col_id, both[:, 0:count], 0.0), both[:, count:], weak


def finish_kernel(
    total,
    mine_ref,
    other_ref,
    placed_ref,
    basis_ref,
    modes_hbm,
    coeffs_hbm,
    upper_ref,
    weak_ref,
    sums_ref,
    coeffs_ref,
    resid_ref,
    modes_ref,
    coeffs_sem,
    modes_sems,
):
    snapcount, cells = placed_ref.shape
    rank = basis_ref.shape[1]
    cell_total = cells * total
    half, quarter = rank // 2, rank // 4
    share = mine_ref.shape[0]
    first = parity(device_index(), total) == 0
    sums_ref[0:share] = jnp.where(first, mine_ref[...], other_ref[...])
    sums_ref[share:] = jnp.where(first, other_ref[...], mine_ref[...])
    fold_rows = 3 * quarter + half
    parts = rank // LANES
    raw = jnp.concatenate(
        [sums_ref[fold_rows + k * snapcount : fold_rows + (k + 1) * snapcount] for k in range(parts)],
        axis=1,
    )
    at = fold_rows + parts * snapcount
    own = sums_ref[at : at + snapcount, 0:snapcount]
    coeffs = raw / cell_total
    coeffs_ref[...] = coeffs
    coeffs_copy = pltpu.make_async_copy(coeffs_ref, coeffs_hbm, coeffs_sem)
    coeffs_copy.start()
    narrow = coeffs.astype(jnp.bfloat16)
    rounded = narrow.astype(F32)

    upper = lane_at_least((quarter, half), quarter)
    middle = sums_ref[quarter : 2 * quarter]
    left = jnp.concatenate([sums_ref[0:quarter], jnp.where(upper, middle, 0.0)], axis=0)
    right = jnp.concatenate(
        [
            sums_ref[3 * quarter : fold_rows],
            jnp.where(upper, 0.0, middle),
            sums_ref[2 * quarter : 3 * quarter],
        ],
        axis=0,
    )
    spread = jnp.concatenate(
        [
            jnp.dot(rounded[:, 0:half], left, precision=HIGH, preferred_element_type=F32),
            jnp.dot(rounded, right, precision=HIGH, preferred_element_type=F32),
        ],
        axis=1,
    )
    cross = nt(raw, rounded, HIGH)
    quad = nt(spread, rounded, HIGH)
    gram = (own - (cross + cross.T) + 0.5 * (quad + quad.T)) / cell_total
    size = own + 2.0 * jnp.abs(cross) + jnp.abs(quad)
    eye = lax.broadcasted_iota(jnp.int32, size.shape, 0) == lax.broadcasted_iota(
        jnp.int32, size.shape, 1
    )
    scale = jnp.sum(jnp.where(eye, size, 0.0), axis=1, keepdims=True) / cell_total
    upper_factor, inverse, weak = factor(gram, scale)
    upper_ref[...] = upper_factor
    weak_ref[0] = weak
    columns = [jnp.broadcast_to(column(inverse, row), (snapcount, LANES)) for row in range(snapcount)]

    stretch = cells // STRETCHES
    outgoing = []
    for index in range(STRETCHES):
        low = index * stretch
        fitted = nt(narrow, basis_ref[low : low + stretch])
        resid_ref[:, low : low + stretch] = (
            placed_ref[:, low : low + stretch].astype(F32) - fitted
        )
        for lane in range(low, low + stretch, LANES):
            modes = columns[0] * resid_ref[0:1, lane : lane + LANES]
            for row in range(1, snapcount):
                modes += columns[row] * resid_ref[row : row + 1, lane : lane + LANES]
            modes_ref[:, lane : lane + LANES] = modes.astype(jnp.bfloat16)
        part = pl.ds(low, stretch)
        outgoing.append(
            pltpu.make_async_copy(modes_ref.at[:, part], modes_hbm.at[:, part], modes_sems.at[index])
        )
        outgoing[index].start()
    coeffs_copy.wait()
    for copy in outgoing:
        copy.wait()


def exchange(value, total, masks):
    def partner(index):
        return index ^ masks[bin(index).count("1") % 2]

    return lax.ppermute(value, AXES, [(index, partner(index)) for index in range(total)])


def flips(count):
    return [(1 << bit) | 1 for bit in range(1, count.bit_length() - 1)]


def all_sum(value, total):
    for mask in [1] + flips(total):
        value = value + exchange(value, total, (mask, mask))
    return value


def kernel_call(kernel, outputs, in_specs, out_specs, scratch=(), **options):
    return pl.pallas_call(
        kernel,
        out_shape=outputs,
        in_specs=in_specs,
        out_specs=out_specs,
        scratch_shapes=scratch,
        compiler_params=pltpu.CompilerParams(vmem_limit_bytes=LIMIT),
        **options,
    )


def spread_boxes(own, peer, groups, total):
    like = jax.ShapeDtypeStruct
    kept, sources = [0], [0, 1]
    for mask in flips(groups):
        kept = kept + [offset ^ mask for offset in kept]
    half = len(kept) // 2
    shape = like((2, half) + own.shape[1:], own.dtype)
    keep, send = kernel_call(
        lambda *refs: pack_kernel(kept, *refs), (shape, shape), [VMEM, VMEM], (VMEM, VMEM)
    )(own, peer)
    for mask in reversed(flips(groups)):
        far = exchange(send, total, (mask, mask))
        sources = sources + [source ^ mask for source in sources]
        if half == 1:
            return keep[:, 0], far[:, 0], sources
        both = jnp.concatenate([keep, far], axis=0)
        half //= 2
        keep, send = both[:, :half], both[:, half:]


def gram_cost(rows, rank):
    return pl.CostEstimate(
        flops=2 * rows * rank * rank, bytes_accessed=2 * rows * rank, transcendentals=0
    )


def local(snaps_box, box_order, basis):
    like = jax.ShapeDtypeStruct
    snapcount = snaps_box.shape[0]
    local_cells, rank = basis.shape
    groups = lax.axis_size("sub")
    total = lax.axis_size("rows") * groups
    block_len = local_cells // groups
    cell_total = local_cells * total

    boxes = snaps_box.reshape(snapcount, groups, block_len).transpose(1, 0, 2)
    peer = exchange(boxes, total, (1, 1))
    eighth = local_cells // 8
    done = 2 * eighth
    rest = [(done, 3 * eighth), (3 * eighth, 5 * eighth), (5 * eighth, local_cells)]
    held = like(basis.shape, basis.dtype)
    own, near, total_gram = kernel_call(
        lambda *refs: open_kernel(done, *refs),
        (like(boxes.shape, boxes.dtype), held, like((rank, rank), F32)),
        [HBM, HBM],
        (VMEM, VMEM, VMEM),
        [DMA(()), DMA((1,))],
        cost_estimate=gram_cost(done, rank),
    )(boxes, basis)
    keep, far, sources = spread_boxes(own, peer, groups, total)

    half, quarter = rank // 2, rank // 4
    fold_rows = 3 * quarter + half
    fold, near = kernel_call(
        lambda *refs: gram_kernel(rest, *refs),
        (like((fold_rows, half), F32), held),
        [HBM, VMEM, VMEM],
        (VMEM, VMEM),
        [DMA((len(rest),))],
        input_output_aliases={1: 1},
        cost_estimate=gram_cost(local_cells - done, rank),
    )(basis, near, total_gram)
    used = fold_rows + (rank // LANES + 1) * snapcount
    share = -(-used // 16) * 8
    part = like((share, LANES), F32)
    mine, send, placed = kernel_call(
        lambda *refs: project_kernel(sources, total, *refs),
        (part, part, like((snapcount, local_cells), snaps_box.dtype)),
        [ANY, VMEM, VMEM, VMEM, VMEM],
        (VMEM, VMEM, VMEM),
        [
            pltpu.VMEM((2 * share, LANES), F32),
            pltpu.SMEM(box_order.shape, box_order.dtype),
            DMA(()),
        ],
    )(box_order, keep, far, near, fold)

    mine = mine + exchange(send, total, (1, 1))
    masks = flips(total)
    swapped = list(masks)
    for index in range(0, len(masks) - 1, 2):
        swapped[index], swapped[index + 1] = masks[index + 1], masks[index]
    for pair in zip(masks, swapped):
        mine = mine + exchange(mine, total, pair)
    other = exchange(mine, total, (1, 1))

    modes, coeffs, r_factor, weak = kernel_call(
        lambda *refs: finish_kernel(total, *refs),
        (
            like((snapcount, local_cells), jnp.bfloat16),
            like((snapcount, rank), F32),
            like((snapcount, snapcount), F32),
            like((1,), F32),
        ),
        [VMEM, VMEM, VMEM, VMEM],
        (HBM, HBM, VMEM, SMEM),
        [
            pltpu.VMEM((2 * share, LANES), F32),
            pltpu.VMEM((snapcount, rank), F32),
            pltpu.VMEM((snapcount, local_cells), F32),
            pltpu.VMEM((snapcount, local_cells), jnp.bfloat16),
            DMA(()),
            DMA((STRETCHES,)),
        ],
    )(mine, other, placed, near)

    def direct(_):
        residual = placed.astype(F32) - nt(coeffs.astype(jnp.bfloat16), basis)
        wgram = all_sum(jnp.dot(residual, residual.T, precision=HIGH) / cell_total, total)
        lower = jnp.linalg.cholesky(wgram)
        solved = jax.scipy.linalg.solve_triangular(lower, residual, lower=True)
        return solved.astype(jnp.bfloat16), lower.T

    modes, r_factor = lax.cond(weak[0] > 0.0, direct, lambda ready: ready, (modes, r_factor))
    return modes, coeffs, r_factor


def solution(mesh):
    return jax.shard_map(
        local,
        mesh=mesh,
        in_specs=(P(None, AXES), P("rows", None, None), P(AXES, None)),
        out_specs=(P(None, AXES), P(), P()),
        check_vma=False,
    )
```

```python
import jax
import jax.numpy as jnp
from jax import lax
from jax.experimental import pallas as pl
from jax.experimental.pallas import tpu as pltpu
from jax.sharding import PartitionSpec as P

AXES = ("rows", "sub")
HIGH = lax.Precision.HIGHEST
LANES = 128
GUARD = 1.0 / 64.0
STRETCHES = 8
HBM = pl.BlockSpec(memory_space=pltpu.HBM)
ANY = pl.BlockSpec(memory_space=pl.ANY)
DMA = pltpu.SemaphoreType.DMA
LIMIT = 16 * 1048576
VMEM = pl.BlockSpec(memory_space=pltpu.VMEM)
SMEM = pl.BlockSpec(memory_space=pltpu.SMEM)
F32 = jnp.float32


def nt(a, b, precision=None):
    return lax.dot_general(
        a, b, (((1,), (1,)), ((), ())), precision=precision, preferred_element_type=F32
    )


def lane_at_least(shape, bound):
    return lax.broadcasted_iota(jnp.int32, shape, len(shape) - 1) >= bound


def gram_of(part):
    return lax.dot_general(part, part, (((0,), (0,)), ((), ())), preferred_element_type=F32)


def fetch_kernel(far_ref, near_ref, sem):
    copy = pltpu.make_async_copy(far_ref, near_ref, sem)
    copy.start()
    copy.wait()


def gram_kernel(bounds, basis_ref, fold_ref, near_ref, sems):
    rank = near_ref.shape[1]
    half, quarter = rank // 2, rank // 4
    moves = []
    for index, (low, high) in enumerate(bounds):
        part = pl.ds(low, high - low)
        moves.append(
            pltpu.make_async_copy(basis_ref.at[part], near_ref.at[part], sems.at[index])
        )
        moves[index].start()
    total = jnp.zeros((rank, rank), F32)
    for move, (low, high) in zip(moves, bounds):
        move.wait()
        total += gram_of(near_ref[low:high])
    upper = lane_at_least((quarter, half), quarter)
    fold_ref[0:quarter] = jnp.where(upper, 2.0, 1.0) * total[0:quarter, 0:half]
    fold_ref[quarter : 2 * quarter] = jnp.where(
        upper, total[quarter:half, 0:half], total[half : 3 * quarter, half:]
    )
    fold_ref[2 * quarter : 3 * quarter] = jnp.where(upper, 1.0, 2.0) * total[3 * quarter :, half:]
    fold_ref[3 * quarter : 3 * quarter + half] = 2.0 * total[0:half, half:]


def device_index():
    return lax.axis_index("rows") * lax.axis_size("sub") + lax.axis_index("sub")


def parity(device, total):
    value = device
    for bit in range(1, (total - 1).bit_length()):
        value = value ^ (device >> bit)
    return value & 1


def pack_kernel(kept, own_ref, peer_ref, keep_ref, send_ref):
    position = lax.axis_index("sub")
    half = len(kept) // 2
    for source, ref in enumerate((own_ref, peer_ref)):
        for index, offset in enumerate(kept):
            out = keep_ref if index < half else send_ref
            out[source, index % half] = ref[position ^ offset]


def project_kernel(
    sources,
    total,
    order_hbm,
    keep_ref,
    far_ref,
    basis_ref,
    fold_ref,
    mine_ref,
    send_ref,
    placed_ref,
    out_ref,
    order_ref,
    sem,
):
    table = pltpu.make_async_copy(order_hbm, order_ref, sem)
    table.start()
    near, snapcount, block_len = keep_ref.shape
    share = mine_ref.shape[0]
    fold_rows = fold_ref.shape[0]
    rank = basis_ref.shape[1]
    blocks = [keep_ref[index] for index in range(near)]
    blocks += [far_ref[index] for index in range(len(sources) - near)]
    out_ref[0:fold_rows] = fold_ref[...]
    own = nt(blocks[0], blocks[0])
    for block in blocks[1:]:
        own += nt(block, block)
    table.wait()
    position = lax.axis_index("sub")
    raw = jnp.zeros((snapcount, rank), F32)
    for source, block in zip(sources, blocks):
        start = order_ref[0, position, position ^ source] * block_len
        start = pl.multiple_of(start, block_len)
        raw += jnp.dot(block, basis_ref[pl.ds(start, block_len), :], preferred_element_type=F32)
        placed_ref[:, pl.ds(start, block_len)] = block
    at = fold_rows
    for part in range(rank // LANES):
        out_ref[at : at + snapcount] = raw[:, part * LANES : (part + 1) * LANES]
        at += snapcount
    out_ref[at:] = jnp.zeros((out_ref.shape[0] - at, LANES), F32)
    out_ref[at : at + snapcount, 0:snapcount] = own
    side = parity(device_index(), total)
    mine_ref[...] = out_ref[pl.ds(pl.multiple_of(side * share, 8), share)]
    send_ref[...] = out_ref[pl.ds(pl.multiple_of((1 - side) * share, 8), share)]


def column(matrix, index):
    return matrix[:, index : index + 1]


def factor(gram, scale):
    count = gram.shape[0]
    row_id = lax.broadcasted_iota(jnp.int32, (count, count), 0)
    col_id = lax.broadcasted_iota(jnp.int32, (count, count), 1)
    eye = (row_id == col_id).astype(F32)
    both = jnp.concatenate([gram, eye], axis=1)
    rows = lax.broadcasted_iota(jnp.int32, both.shape, 0)
    for step in range(count - 1):
        factors = column(both, step)
        ratio = factors / factors[step : step + 1]
        both -= jnp.where(rows > step, ratio * both[step : step + 1], 0.0)
    pivots = jnp.sum(both[:, 0:count] * eye, axis=1, keepdims=True)
    weak = jnp.sum(jnp.where(pivots >= GUARD * scale, 0.0, 1.0))
    both = both / jnp.sqrt(pivots)
    return jnp.where(row_id <= col_id, both[:, 0:count], 0.0), both[:, count:], weak


def finish_kernel(
    total,
    mine_ref,
    other_ref,
    placed_ref,
    basis_ref,
    modes_hbm,
    coeffs_hbm,
    upper_ref,
    weak_ref,
    sums_ref,
    coeffs_ref,
    resid_ref,
    modes_ref,
    coeffs_sem,
    modes_sems,
):
    snapcount, cells = placed_ref.shape
    rank = basis_ref.shape[1]
    cell_total = cells * total
    half, quarter = rank // 2, rank // 4
    share = mine_ref.shape[0]
    first = parity(device_index(), total) == 0
    sums_ref[0:share] = jnp.where(first, mine_ref[...], other_ref[...])
    sums_ref[share:] = jnp.where(first, other_ref[...], mine_ref[...])
    fold_rows = 3 * quarter + half
    parts = rank // LANES
    raw = jnp.concatenate(
        [sums_ref[fold_rows + k * snapcount : fold_rows + (k + 1) * snapcount] for k in range(parts)],
        axis=1,
    )
    at = fold_rows + parts * snapcount
    own = sums_ref[at : at + snapcount, 0:snapcount]
    coeffs = raw / cell_total
    coeffs_ref[...] = coeffs
    coeffs_copy = pltpu.make_async_copy(coeffs_ref, coeffs_hbm, coeffs_sem)
    coeffs_copy.start()
    narrow = coeffs.astype(jnp.bfloat16)
    rounded = narrow.astype(F32)

    upper = lane_at_least((quarter, half), quarter)
    middle = sums_ref[quarter : 2 * quarter]
    left = jnp.concatenate([sums_ref[0:quarter], jnp.where(upper, middle, 0.0)], axis=0)
    right = jnp.concatenate(
        [
            sums_ref[3 * quarter : fold_rows],
            jnp.where(upper, 0.0, middle),
            sums_ref[2 * quarter : 3 * quarter],
        ],
        axis=0,
    )
    spread = jnp.concatenate(
        [
            jnp.dot(rounded[:, 0:half], left, precision=HIGH, preferred_element_type=F32),
            jnp.dot(rounded, right, precision=HIGH, preferred_element_type=F32),
        ],
        axis=1,
    )
    cross = nt(raw, rounded, HIGH)
    quad = nt(spread, rounded, HIGH)
    gram = (own - (cross + cross.T) + 0.5 * (quad + quad.T)) / cell_total
    size = own + 2.0 * jnp.abs(cross) + jnp.abs(quad)
    eye = lax.broadcasted_iota(jnp.int32, size.shape, 0) == lax.broadcasted_iota(
        jnp.int32, size.shape, 1
    )
    scale = jnp.sum(jnp.where(eye, size, 0.0), axis=1, keepdims=True) / cell_total
    upper_factor, inverse, weak = factor(gram, scale)
    upper_ref[...] = upper_factor
    weak_ref[0] = weak
    columns = [jnp.broadcast_to(column(inverse, row), (snapcount, LANES)) for row in range(snapcount)]

    stretch = cells // STRETCHES
    outgoing = []
    for index in range(STRETCHES):
        low = index * stretch
        fitted = nt(narrow, basis_ref[low : low + stretch])
        resid_ref[:, low : low + stretch] = (
            placed_ref[:, low : low + stretch].astype(F32) - fitted
        )
        for lane in range(low, low + stretch, LANES):
            modes = columns[0] * resid_ref[0:1, lane : lane + LANES]
            for row in range(1, snapcount):
                modes += columns[row] * resid_ref[row : row + 1, lane : lane + LANES]
            modes_ref[:, lane : lane + LANES] = modes.astype(jnp.bfloat16)
        part = pl.ds(low, stretch)
        outgoing.append(
            pltpu.make_async_copy(modes_ref.at[:, part], modes_hbm.at[:, part], modes_sems.at[index])
        )
        outgoing[index].start()
    coeffs_copy.wait()
    for copy in outgoing:
        copy.wait()


def exchange(value, total, masks):
    def partner(index):
        return index ^ masks[bin(index).count("1") % 2]

    return lax.ppermute(value, AXES, [(index, partner(index)) for index in range(total)])


def flips(count):
    return [(1 << bit) | 1 for bit in range(1, count.bit_length() - 1)]


def all_sum(value, total):
    for mask in [1] + flips(total):
        value = value + exchange(value, total, (mask, mask))
    return value


def kernel_call(kernel, outputs, in_specs, out_specs, scratch=(), **options):
    return pl.pallas_call(
        kernel,
        out_shape=outputs,
        in_specs=in_specs,
        out_specs=out_specs,
        scratch_shapes=scratch,
        compiler_params=pltpu.CompilerParams(vmem_limit_bytes=LIMIT),
        **options,
    )


def spread_boxes(own, peer, groups, total):
    like = jax.ShapeDtypeStruct
    kept, sources = [0], [0, 1]
    for mask in flips(groups):
        kept = kept + [offset ^ mask for offset in kept]
    half = len(kept) // 2
    shape = like((2, half) + own.shape[1:], own.dtype)
    keep, send = kernel_call(
        lambda *refs: pack_kernel(kept, *refs), (shape, shape), [VMEM, VMEM], (VMEM, VMEM)
    )(own, peer)
    for mask in reversed(flips(groups)):
        far = exchange(send, total, (mask, mask))
        sources = sources + [source ^ mask for source in sources]
        if half == 1:
            return keep[:, 0], far[:, 0], sources
        both = jnp.concatenate([keep, far], axis=0)
        half //= 2
        keep, send = both[:, :half], both[:, half:]


def gram_cost(rows, rank):
    return pl.CostEstimate(
        flops=2 * rows * rank * rank, bytes_accessed=2 * rows * rank, transcendentals=0
    )


def local(snaps_box, box_order, basis):
    like = jax.ShapeDtypeStruct
    snapcount = snaps_box.shape[0]
    local_cells, rank = basis.shape
    groups = lax.axis_size("sub")
    total = lax.axis_size("rows") * groups
    block_len = local_cells // groups
    cell_total = local_cells * total

    boxes = snaps_box.reshape(snapcount, groups, block_len).transpose(1, 0, 2)
    peer = exchange(boxes, total, (1, 1))
    own = kernel_call(
        fetch_kernel,
        like(boxes.shape, boxes.dtype),
        [HBM],
        VMEM,
        [DMA(())],
        cost_estimate=gram_cost(local_cells, rank),
    )(boxes)
    keep, far, sources = spread_boxes(own, peer, groups, total)

    half, quarter = rank // 2, rank // 4
    fold_rows = 3 * quarter + half
    eighth = local_cells // 8
    bounds = [(0, eighth), (eighth, 3 * eighth), (3 * eighth, local_cells)]
    fold, near = kernel_call(
        lambda *refs: gram_kernel(bounds, *refs),
        (like((fold_rows, half), F32), like(basis.shape, basis.dtype)),
        [HBM],
        (VMEM, VMEM),
        [DMA((len(bounds),))],
        cost_estimate=gram_cost(local_cells, rank),
    )(basis)
    used = fold_rows + (rank // LANES + 1) * snapcount
    share = -(-used // 16) * 8
    part = like((share, LANES), F32)
    mine, send, placed = kernel_call(
        lambda *refs: project_kernel(sources, total, *refs),
        (part, part, like((snapcount, local_cells), snaps_box.dtype)),
        [ANY, VMEM, VMEM, VMEM, VMEM],
        (VMEM, VMEM, VMEM),
        [
            pltpu.VMEM((2 * share, LANES), F32),
            pltpu.SMEM(box_order.shape, box_order.dtype),
            DMA(()),
        ],
    )(box_order, keep, far, near, fold)

    mine = mine + exchange(send, total, (1, 1))
    masks = flips(total)
    swapped = list(masks)
    for index in range(0, len(masks) - 1, 2):
        swapped[index], swapped[index + 1] = masks[index + 1], masks[index]
    for pair in zip(masks, swapped):
        mine = mine + exchange(mine, total, pair)
    other = exchange(mine, total, (1, 1))

    modes, coeffs, r_factor, weak = kernel_call(
        lambda *refs: finish_kernel(total, *refs),
        (
            like((snapcount, local_cells), jnp.bfloat16),
            like((snapcount, rank), F32),
            like((snapcount, snapcount), F32),
            like((1,), F32),
        ),
        [VMEM, VMEM, VMEM, VMEM],
        (HBM, HBM, VMEM, SMEM),
        [
            pltpu.VMEM((2 * share, LANES), F32),
            pltpu.VMEM((snapcount, rank), F32),
            pltpu.VMEM((snapcount, local_cells), F32),
            pltpu.VMEM((snapcount, local_cells), jnp.bfloat16),
            DMA(()),
            DMA((STRETCHES,)),
        ],
    )(mine, other, placed, near)

    def direct(_):
        residual = placed.astype(F32) - nt(coeffs.astype(jnp.bfloat16), basis)
        wgram = all_sum(jnp.dot(residual, residual.T, precision=HIGH) / cell_total, total)
        lower = jnp.linalg.cholesky(wgram)
        solved = jax.scipy.linalg.solve_triangular(lower, residual, lower=True)
        return solved.astype(jnp.bfloat16), lower.T

    modes, r_factor = lax.cond(weak[0] > 0.0, direct, lambda ready: ready, (modes, r_factor))
    return modes, coeffs, r_factor


def solution(mesh):
    return jax.shard_map(
        local,
        mesh=mesh,
        in_specs=(P(None, AXES), P("rows", None, None), P(AXES, None)),
        out_specs=(P(None, AXES), P(), P()),
        check_vma=False,
    )
```

```python
import jax
import jax.numpy as jnp
from jax import lax
from jax.experimental import pallas as pl
from jax.experimental.pallas import tpu as pltpu
from jax.sharding import PartitionSpec as P

AXES = ("rows", "sub")
HIGH = lax.Precision.HIGHEST
LANES, SUBLANES = 128, 8
GUARD = 1.0 / 64.0
STRETCHES = 8
HBM = pl.BlockSpec(memory_space=pltpu.HBM)
ANY = pl.BlockSpec(memory_space=pl.ANY)
DMA = pltpu.SemaphoreType.DMA
LIMIT = 16 * 1048576
VMEM = pl.BlockSpec(memory_space=pltpu.VMEM)
SMEM = pl.BlockSpec(memory_space=pltpu.SMEM)
F32 = jnp.float32


def nt(a, b, precision=None):
    return lax.dot_general(
        a, b, (((1,), (1,)), ((), ())), precision=precision, preferred_element_type=F32
    )


def gram_of(part):
    return lax.dot_general(part, part, (((0,), (0,)), ((), ())), preferred_element_type=F32)


def fetch_kernel(far_ref, near_ref, sem):
    copy = pltpu.make_async_copy(far_ref, near_ref, sem)
    copy.start()
    copy.wait()


def triangle(count):
    shape = (count, count)
    return (
        lax.broadcasted_iota(jnp.int32, shape, 0),
        lax.broadcasted_iota(jnp.int32, shape, 1),
    )


def place_of(order_ref, source):
    position = lax.axis_index("sub")
    order = order_ref[0].astype(F32)
    rows = lax.broadcasted_iota(jnp.int32, order.shape, 0)
    cols = lax.broadcasted_iota(jnp.int32, order.shape, 1)
    wanted = (rows == position) & (cols == position ^ source)
    return jnp.sum(jnp.where(wanted, order, 0.0)).astype(jnp.int32)


def block_sums(sources, order_ref, blocks_ref, basis_ref, placed_ref):
    _, snapcount, block_len = blocks_ref.shape
    raw = jnp.zeros((snapcount, basis_ref.shape[1]), F32)
    own = jnp.zeros((snapcount, snapcount), F32)
    for index, source in enumerate(sources):
        block = blocks_ref[index]
        own += nt(block, block)
        start = pl.multiple_of(place_of(order_ref, source) * block_len, block_len)
        raw += jnp.dot(block, basis_ref[pl.ds(start, block_len), :], preferred_element_type=F32)
        placed_ref[:, pl.ds(start, block_len)] = block
    return raw, own


def gram_kernel(
    sources, order_ref, keep_ref, basis_ref, sums_ref, near_ref, placed_ref, sem
):
    move = pltpu.make_async_copy(basis_ref, near_ref, sem)
    move.start()
    move.wait()
    snapcount = keep_ref.shape[1]
    rank = near_ref.shape[1]
    half = rank // 2
    raw, own = block_sums(sources, order_ref, keep_ref, near_ref, placed_ref)
    total = gram_of(near_ref[...])
    row_id, col_id = triangle(half)
    corner = total[half:, half:]
    sums_ref[0:half] = jnp.where(row_id == col_id, 1.0, 2.0) * jnp.where(
        row_id >= col_id, total[0:half, 0:half], corner
    )
    sums_ref[half:rank] = 2.0 * total[0:half, half:]
    edge = jnp.sum(jnp.where(row_id == col_id, corner, 0.0), axis=0, keepdims=True)
    at = rank
    sums_ref[at : at + SUBLANES] = jnp.broadcast_to(edge, (SUBLANES, half))
    at += SUBLANES
    for part in range(rank // half):
        sums_ref[at : at + snapcount] = raw[:, part * half : (part + 1) * half]
        at += snapcount
    sums_ref[at:] = jnp.zeros((sums_ref.shape[0] - at, half), F32)
    sums_ref[at : at + snapcount, 0:snapcount] = own


def device_index():
    return lax.axis_index("rows") * lax.axis_size("sub") + lax.axis_index("sub")


def parity(device, total):
    value = device
    for bit in range(1, (total - 1).bit_length()):
        value = value ^ (device >> bit)
    return value & 1


def pack_kernel(kept, own_ref, peer_ref, keep_ref, send_ref):
    position = lax.axis_index("sub")
    half = len(kept) // 2
    for source, ref in enumerate((own_ref, peer_ref)):
        for index, offset in enumerate(kept):
            out = keep_ref if index < half else send_ref
            out[source, index % half] = ref[position ^ offset]


def project_kernel(
    sources,
    total,
    order_ref,
    far_ref,
    basis_ref,
    sums_ref,
    placed_in,
    mine_ref,
    send_ref,
    placed_ref,
    out_ref,
):
    snapcount = far_ref.shape[1]
    rank = basis_ref.shape[1]
    half = rank // 2
    share = mine_ref.shape[0]
    raw, own = block_sums(sources, order_ref, far_ref, basis_ref, placed_ref)
    out_ref[...] = sums_ref[...]
    at = rank + SUBLANES
    for part in range(rank // half):
        out_ref[at : at + snapcount] += raw[:, part * half : (part + 1) * half]
        at += snapcount
    out_ref[at : at + snapcount, 0:snapcount] += own
    side = parity(device_index(), total)
    mine_ref[...] = out_ref[pl.ds(pl.multiple_of(side * share, SUBLANES), share)]
    send_ref[...] = out_ref[pl.ds(pl.multiple_of((1 - side) * share, SUBLANES), share)]


def column(matrix, index):
    return matrix[:, index : index + 1]


def factor(gram, scale):
    count = gram.shape[0]
    row_id = lax.broadcasted_iota(jnp.int32, (count, count), 0)
    col_id = lax.broadcasted_iota(jnp.int32, (count, count), 1)
    eye = (row_id == col_id).astype(F32)
    both = jnp.concatenate([gram, eye], axis=1)
    rows = lax.broadcasted_iota(jnp.int32, both.shape, 0)
    for step in range(count - 1):
        factors = column(both, step)
        ratio = factors / factors[step : step + 1]
        both -= jnp.where(rows > step, ratio * both[step : step + 1], 0.0)
    pivots = jnp.sum(both[:, 0:count] * eye, axis=1, keepdims=True)
    weak = jnp.sum(jnp.where(pivots >= GUARD * scale, 0.0, 1.0))
    both = both / jnp.sqrt(pivots)
    return jnp.where(row_id <= col_id, both[:, 0:count], 0.0), both[:, count:], weak


def finish_kernel(
    total,
    mine_ref,
    other_ref,
    placed_ref,
    basis_ref,
    modes_ref,
    coeffs_ref,
    upper_ref,
    weak_ref,
    sums_ref,
    resid_ref,
):
    snapcount, cells = placed_ref.shape
    rank = basis_ref.shape[1]
    cell_total = cells * total
    half = rank // 2
    share = mine_ref.shape[0]
    first = parity(device_index(), total) == 0
    sums_ref[0:share] = jnp.where(first, mine_ref[...], other_ref[...])
    sums_ref[share:] = jnp.where(first, other_ref[...], mine_ref[...])
    at = rank + SUBLANES
    parts = []
    for _ in range(rank // half):
        parts.append(sums_ref[at : at + snapcount])
        at += snapcount
    raw = jnp.concatenate(parts, axis=1)
    own = sums_ref[at : at + snapcount, 0:snapcount]
    coeffs = raw / cell_total
    coeffs_ref[...] = coeffs
    narrow = coeffs.astype(jnp.bfloat16)
    rounded = narrow.astype(F32)

    row_id, col_id = triangle(half)
    square = sums_ref[0:half]
    left = jnp.where(row_id >= col_id, square, 0.0)
    right = jnp.concatenate(
        [sums_ref[half:rank], jnp.where(row_id < col_id, square, 0.0)], axis=0
    )
    edge = sums_ref[rank : rank + 1]
    spread = jnp.concatenate(
        [
            jnp.dot(rounded[:, 0:half], left, precision=HIGH, preferred_element_type=F32),
            jnp.dot(rounded, right, precision=HIGH, preferred_element_type=F32)
            + rounded[:, half:] * edge,
        ],
        axis=1,
    )
    cross = nt(raw, rounded, HIGH)
    quad = nt(spread, rounded, HIGH)
    gram = (own - (cross + cross.T) + 0.5 * (quad + quad.T)) / cell_total
    size = own + 2.0 * jnp.abs(cross) + jnp.abs(quad)
    eye = lax.broadcasted_iota(jnp.int32, size.shape, 0) == lax.broadcasted_iota(
        jnp.int32, size.shape, 1
    )
    scale = jnp.sum(jnp.where(eye, size, 0.0), axis=1, keepdims=True) / cell_total
    upper_factor, inverse, weak = factor(gram, scale)
    upper_ref[...] = upper_factor
    weak_ref[0] = weak
    columns = [jnp.broadcast_to(column(inverse, row), (snapcount, LANES)) for row in range(snapcount)]

    stretch = cells // STRETCHES
    for index in range(STRETCHES):
        low = index * stretch
        fitted = nt(narrow, basis_ref[low : low + stretch])
        resid_ref[:, low : low + stretch] = (
            placed_ref[:, low : low + stretch].astype(F32) - fitted
        )
        for lane in range(low, low + stretch, LANES):
            modes = columns[0] * resid_ref[0:1, lane : lane + LANES]
            for row in range(1, snapcount):
                modes += columns[row] * resid_ref[row : row + 1, lane : lane + LANES]
            modes_ref[:, lane : lane + LANES] = modes.astype(jnp.bfloat16)


def exchange(value, total, masks):
    def partner(index):
        return index ^ masks[bin(index).count("1") % 2]

    return lax.ppermute(value, AXES, [(index, partner(index)) for index in range(total)])


def flips(count):
    return [(1 << bit) | 1 for bit in range(1, count.bit_length() - 1)]


def all_sum(value, total):
    for mask in [1] + flips(total):
        value = value + exchange(value, total, (mask, mask))
    return value


def kernel_call(kernel, outputs, in_specs, out_specs, scratch=(), **options):
    return pl.pallas_call(
        kernel,
        out_shape=outputs,
        in_specs=in_specs,
        out_specs=out_specs,
        scratch_shapes=scratch,
        compiler_params=pltpu.CompilerParams(vmem_limit_bytes=LIMIT),
        **options,
    )


def spread_boxes(own, peer, groups, total):
    like = jax.ShapeDtypeStruct
    kept, sources = [0], [0, 1]
    for mask in flips(groups):
        kept = kept + [offset ^ mask for offset in kept]
    half = len(kept) // 2
    shape = like((2, half) + own.shape[1:], own.dtype)
    keep, send = kernel_call(
        lambda *refs: pack_kernel(kept, *refs), (shape, shape), [VMEM, VMEM], (VMEM, VMEM)
    )(own, peer)
    for mask in reversed(flips(groups)):
        far = exchange(send, total, (mask, mask))
        sources = sources + [source ^ mask for source in sources]
        if half == 1:
            return keep[:, 0], far[:, 0], sources
        both = jnp.concatenate([keep, far], axis=0)
        half //= 2
        keep, send = both[:, :half], both[:, half:]


def gram_cost(rows, rank):
    return pl.CostEstimate(
        flops=2 * rows * rank * rank, bytes_accessed=2 * rows * rank, transcendentals=0
    )


def local(snaps_box, box_order, basis):
    like = jax.ShapeDtypeStruct
    snapcount = snaps_box.shape[0]
    local_cells, rank = basis.shape
    groups = lax.axis_size("sub")
    total = lax.axis_size("rows") * groups
    block_len = local_cells // groups
    cell_total = local_cells * total

    boxes = snaps_box.reshape(snapcount, groups, block_len).transpose(1, 0, 2)
    peer = exchange(boxes, total, (1, 1))
    own = kernel_call(
        fetch_kernel,
        like(boxes.shape, boxes.dtype),
        [HBM],
        VMEM,
        [DMA(())],
        cost_estimate=gram_cost(local_cells, rank),
    )(boxes)
    keep, far, sources = spread_boxes(own, peer, groups, total)

    half = rank // 2
    used = rank + SUBLANES + (rank // half + 1) * snapcount
    share = -(-used // (2 * SUBLANES)) * SUBLANES
    sums_shape = like((2 * share, half), F32)
    placed_shape = like((snapcount, local_cells), snaps_box.dtype)
    first = keep.shape[0]
    sums, near, placed = kernel_call(
        lambda *refs: gram_kernel(sources[:first], *refs),
        (sums_shape, like(basis.shape, basis.dtype), placed_shape),
        [VMEM, VMEM, HBM],
        (VMEM, VMEM, VMEM),
        [DMA(())],
        cost_estimate=gram_cost(local_cells, rank),
    )(box_order, keep, basis)
    part = like((share, half), F32)
    mine, send, placed = kernel_call(
        lambda *refs: project_kernel(sources[first:], total, *refs),
        (part, part, placed_shape),
        [VMEM, VMEM, VMEM, VMEM, VMEM],
        (VMEM, VMEM, VMEM),
        [pltpu.VMEM(sums_shape.shape, F32)],
        input_output_aliases={4: 2},
    )(box_order, far, near, sums, placed)

    mine = mine + exchange(send, total, (1, 1))
    masks = flips(total)
    swapped = list(masks)
    for index in range(0, len(masks) - 1, 2):
        swapped[index], swapped[index + 1] = masks[index + 1], masks[index]
    for pair in zip(masks, swapped):
        mine = mine + exchange(mine, total, pair)
    other = exchange(mine, total, (1, 1))

    modes, coeffs, r_factor, weak = kernel_call(
        lambda *refs: finish_kernel(total, *refs),
        (
            like((snapcount, local_cells), jnp.bfloat16),
            like((snapcount, rank), F32),
            like((snapcount, snapcount), F32),
            like((1,), F32),
        ),
        [VMEM, VMEM, VMEM, VMEM],
        (VMEM, VMEM, VMEM, SMEM),
        [
            pltpu.VMEM(sums_shape.shape, F32),
            pltpu.VMEM((snapcount, local_cells), F32),
        ],
    )(mine, other, placed, near)

    def direct(_):
        residual = placed.astype(F32) - nt(coeffs.astype(jnp.bfloat16), basis)
        wgram = all_sum(jnp.dot(residual, residual.T, precision=HIGH) / cell_total, total)
        lower = jnp.linalg.cholesky(wgram)
        solved = jax.scipy.linalg.solve_triangular(lower, residual, lower=True)
        return solved.astype(jnp.bfloat16), lower.T

    modes, r_factor = lax.cond(weak[0] > 0.0, direct, lambda ready: ready, (modes, r_factor))
    return modes, coeffs, r_factor


def solution(mesh):
    return jax.shard_map(
        local,
        mesh=mesh,
        in_specs=(P(None, AXES), P("rows", None, None), P(AXES, None)),
        out_specs=(P(None, AXES), P(), P()),
        check_vma=False,
    )
```

```python
import jax
import jax.numpy as jnp
from jax import lax
from jax._src.lax.control_flow.conditionals import _switch_internal
from jax.experimental import pallas as pl
from jax.experimental.pallas import tpu as pltpu
from jax.sharding import PartitionSpec as P

AXES = ("rows", "sub")
HIGH = lax.Precision.HIGHEST
LANES, SUBLANES = 128, 8
GUARD = 1.0 / 64.0
STRETCHES = 8
HBM = pl.BlockSpec(memory_space=pltpu.HBM)
ANY = pl.BlockSpec(memory_space=pl.ANY)
DMA = pltpu.SemaphoreType.DMA
LIMIT = 16 * 1048576
VMEM = pl.BlockSpec(memory_space=pltpu.VMEM)
SMEM = pl.BlockSpec(memory_space=pltpu.SMEM)
F32 = jnp.float32


def nt(a, b, precision=None):
    return lax.dot_general(
        a, b, (((1,), (1,)), ((), ())), precision=precision, preferred_element_type=F32
    )


def gram_of(part):
    return lax.dot_general(part, part, (((0,), (0,)), ((), ())), preferred_element_type=F32)


def fetch_kernel(far_ref, near_ref, sem):
    copy = pltpu.make_async_copy(far_ref, near_ref, sem)
    copy.start()
    copy.wait()


def triangle(count):
    shape = (count, count)
    return (
        lax.broadcasted_iota(jnp.int32, shape, 0),
        lax.broadcasted_iota(jnp.int32, shape, 1),
    )


def place_of(order_ref, source):
    position = lax.axis_index("sub")
    order = order_ref[0].astype(F32)
    rows = lax.broadcasted_iota(jnp.int32, order.shape, 0)
    cols = lax.broadcasted_iota(jnp.int32, order.shape, 1)
    wanted = (rows == position) & (cols == position ^ source)
    return jnp.sum(jnp.where(wanted, order, 0.0)).astype(jnp.int32)


def block_sums(sources, order_ref, blocks_ref, basis_ref, placed_ref):
    _, snapcount, block_len = blocks_ref.shape
    raw = jnp.zeros((snapcount, basis_ref.shape[1]), F32)
    own = jnp.zeros((snapcount, snapcount), F32)
    for index, source in enumerate(sources):
        block = blocks_ref[index]
        own += nt(block, block)
        start = pl.multiple_of(place_of(order_ref, source) * block_len, block_len)
        raw += jnp.dot(block, basis_ref[pl.ds(start, block_len), :], preferred_element_type=F32)
        placed_ref[:, pl.ds(start, block_len)] = block
    return raw, own


def gram_kernel(
    sources, order_ref, keep_ref, basis_ref, sums_ref, near_ref, placed_ref, sem
):
    move = pltpu.make_async_copy(basis_ref, near_ref, sem)
    move.start()
    move.wait()
    snapcount = keep_ref.shape[1]
    rank = near_ref.shape[1]
    half = rank // 2
    raw, own = block_sums(sources, order_ref, keep_ref, near_ref, placed_ref)
    total = gram_of(near_ref[...])
    row_id, col_id = triangle(half)
    corner = total[half:, half:]
    sums_ref[0:half] = jnp.where(row_id == col_id, 1.0, 2.0) * jnp.where(
        row_id >= col_id, total[0:half, 0:half], corner
    )
    sums_ref[half:rank] = 2.0 * total[0:half, half:]
    edge = jnp.sum(jnp.where(row_id == col_id, corner, 0.0), axis=0, keepdims=True)
    at = rank
    sums_ref[at : at + SUBLANES] = jnp.broadcast_to(edge, (SUBLANES, half))
    at += SUBLANES
    for part in range(rank // half):
        sums_ref[at : at + snapcount] = raw[:, part * half : (part + 1) * half]
        at += snapcount
    sums_ref[at:] = jnp.zeros((sums_ref.shape[0] - at, half), F32)
    sums_ref[at : at + snapcount, 0:snapcount] = own


def device_index():
    return lax.axis_index("rows") * lax.axis_size("sub") + lax.axis_index("sub")


def parity(device, total):
    value = device
    for bit in range(1, (total - 1).bit_length()):
        value = value ^ (device >> bit)
    return value & 1


def pack_kernel(kept, own_ref, peer_ref, keep_ref, send_ref):
    position = lax.axis_index("sub")
    half = len(kept) // 2
    for source, ref in enumerate((own_ref, peer_ref)):
        for index, offset in enumerate(kept):
            out = keep_ref if index < half else send_ref
            out[source, index % half] = ref[position ^ offset]


def project_kernel(
    sources,
    total,
    order_ref,
    far_ref,
    basis_ref,
    sums_ref,
    placed_in,
    mine_ref,
    send_ref,
    placed_ref,
    out_ref,
):
    snapcount = far_ref.shape[1]
    rank = basis_ref.shape[1]
    half = rank // 2
    share = mine_ref.shape[0]
    raw, own = block_sums(sources, order_ref, far_ref, basis_ref, placed_ref)
    out_ref[...] = sums_ref[...]
    at = rank + SUBLANES
    for part in range(rank // half):
        out_ref[at : at + snapcount] += raw[:, part * half : (part + 1) * half]
        at += snapcount
    out_ref[at : at + snapcount, 0:snapcount] += own
    side = parity(device_index(), total)
    mine_ref[...] = out_ref[pl.ds(pl.multiple_of(side * share, SUBLANES), share)]
    send_ref[...] = out_ref[pl.ds(pl.multiple_of((1 - side) * share, SUBLANES), share)]


def exact_dot(narrow, wide):
    total = None
    for _ in range(3):
        part = wide.astype(jnp.bfloat16)
        wide = wide - part.astype(F32)
        term = jnp.dot(narrow, part, preferred_element_type=F32)
        total = term if total is None else total + term
    return total


def left_exact_nt(wide, narrow):
    parts = []
    for _ in range(3):
        parts.append(wide.astype(jnp.bfloat16))
        wide = wide - parts[-1].astype(F32)
    stacked = nt(jnp.concatenate(parts, axis=0), narrow)
    count = wide.shape[0]
    return stacked[0:count] + stacked[count : 2 * count] + stacked[2 * count :]


def column(matrix, index):
    return matrix[:, index : index + 1]


def factor(gram, scale):
    count = gram.shape[0]
    row_id = lax.broadcasted_iota(jnp.int32, (count, count), 0)
    col_id = lax.broadcasted_iota(jnp.int32, (count, count), 1)
    eye = (row_id == col_id).astype(F32)
    both = jnp.concatenate([gram, eye], axis=1)
    rows = lax.broadcasted_iota(jnp.int32, both.shape, 0)
    for step in range(count - 1):
        factors = column(both, step)
        ratio = factors / factors[step : step + 1]
        both -= jnp.where(rows > step, ratio * both[step : step + 1], 0.0)
    pivots = jnp.sum(both[:, 0:count] * eye, axis=1, keepdims=True)
    weak = jnp.sum(jnp.where(pivots >= GUARD * scale, 0.0, 1.0), axis=0, keepdims=True)
    both = both / jnp.sqrt(pivots)
    return jnp.where(row_id <= col_id, both[:, 0:count], 0.0), both[:, count:], weak


def finish_kernel(
    total,
    mine_ref,
    other_ref,
    placed_ref,
    basis_ref,
    modes_ref,
    coeffs_ref,
    upper_ref,
    weak_ref,
    sums_ref,
    resid_ref,
):
    snapcount, cells = placed_ref.shape
    rank = basis_ref.shape[1]
    cell_total = cells * total
    half = rank // 2
    share = mine_ref.shape[0]
    first = parity(device_index(), total) == 0
    sums_ref[0:share] = jnp.where(first, mine_ref[...], other_ref[...])
    sums_ref[share:] = jnp.where(first, other_ref[...], mine_ref[...])
    at = rank + SUBLANES
    parts = []
    for _ in range(rank // half):
        parts.append(sums_ref[at : at + snapcount])
        at += snapcount
    raw = jnp.concatenate(parts, axis=1)
    own = sums_ref[at : at + snapcount, 0:snapcount]
    coeffs = raw / cell_total
    coeffs_ref[...] = coeffs
    narrow = coeffs.astype(jnp.bfloat16)
    rounded = narrow.astype(F32)

    row_id, col_id = triangle(half)
    square = sums_ref[0:half]
    left = jnp.where(row_id >= col_id, square, 0.0)
    right = jnp.concatenate(
        [sums_ref[half:rank], jnp.where(row_id < col_id, square, 0.0)], axis=0
    )
    edge = sums_ref[rank : rank + 1]
    spread = jnp.concatenate(
        [
            exact_dot(narrow[:, 0:half], left),
            exact_dot(narrow, right) + rounded[:, half:] * edge,
        ],
        axis=1,
    )
    pull = left_exact_nt(0.5 * spread - raw, narrow)
    gram = (own + pull + pull.T) / cell_total
    eye = lax.broadcasted_iota(jnp.int32, own.shape, 0) == lax.broadcasted_iota(
        jnp.int32, own.shape, 1
    )
    scale = (
        jnp.sum(jnp.where(eye, own, 0.0), axis=1, keepdims=True)
        + 2.0 * jnp.abs(jnp.sum(raw * rounded, axis=1, keepdims=True))
        + jnp.abs(jnp.sum(spread * rounded, axis=1, keepdims=True))
    ) / cell_total
    upper_factor, inverse, weak = factor(gram, scale)
    upper_ref[...] = upper_factor
    weak_ref[...] = (weak > 0.0).astype(jnp.int32)
    columns = [jnp.broadcast_to(column(inverse, row), (snapcount, LANES)) for row in range(snapcount)]

    stretch = cells // STRETCHES
    for index in range(STRETCHES):
        low = index * stretch
        fitted = nt(narrow, basis_ref[low : low + stretch])
        resid_ref[:, low : low + stretch] = (
            placed_ref[:, low : low + stretch].astype(F32) - fitted
        )
        for lane in range(low, low + stretch, LANES):
            modes = columns[0] * resid_ref[0:1, lane : lane + LANES]
            for row in range(1, snapcount):
                modes += columns[row] * resid_ref[row : row + 1, lane : lane + LANES]
            modes_ref[:, lane : lane + LANES] = modes.astype(jnp.bfloat16)


def exchange(value, total, masks):
    def partner(index):
        return index ^ masks[bin(index).count("1") % 2]

    return lax.ppermute(value, AXES, [(index, partner(index)) for index in range(total)])


def flips(count):
    return [(1 << bit) | 1 for bit in range(1, count.bit_length() - 1)]


def all_sum(value, total):
    for mask in [1] + flips(total):
        value = value + exchange(value, total, (mask, mask))
    return value


def kernel_call(kernel, outputs, in_specs, out_specs, scratch=(), **options):
    return pl.pallas_call(
        kernel,
        out_shape=outputs,
        in_specs=in_specs,
        out_specs=out_specs,
        scratch_shapes=scratch,
        compiler_params=pltpu.CompilerParams(vmem_limit_bytes=LIMIT),
        **options,
    )


def spread_boxes(own, peer, groups, total):
    like = jax.ShapeDtypeStruct
    kept, sources = [0], [0, 1]
    for mask in flips(groups):
        kept = kept + [offset ^ mask for offset in kept]
    half = len(kept) // 2
    shape = like((2, half) + own.shape[1:], own.dtype)
    keep, send = kernel_call(
        lambda *refs: pack_kernel(kept, *refs), (shape, shape), [VMEM, VMEM], (VMEM, VMEM)
    )(own, peer)
    for mask in reversed(flips(groups)):
        far = exchange(send, total, (mask, mask))
        sources = sources + [source ^ mask for source in sources]
        if half == 1:
            return keep[:, 0], far[:, 0], sources
        both = jnp.concatenate([keep, far], axis=0)
        half //= 2
        keep, send = both[:, :half], both[:, half:]


def gram_cost(rows, rank):
    return pl.CostEstimate(
        flops=2 * rows * rank * rank, bytes_accessed=2 * rows * rank, transcendentals=0
    )


def local(snaps_box, box_order, basis):
    like = jax.ShapeDtypeStruct
    snapcount = snaps_box.shape[0]
    local_cells, rank = basis.shape
    groups = lax.axis_size("sub")
    total = lax.axis_size("rows") * groups
    block_len = local_cells // groups
    cell_total = local_cells * total

    boxes = snaps_box.reshape(snapcount, groups, block_len).transpose(1, 0, 2)
    peer = exchange(boxes, total, (1, 1))
    own = kernel_call(
        fetch_kernel,
        like(boxes.shape, boxes.dtype),
        [HBM],
        VMEM,
        [DMA(())],
        cost_estimate=gram_cost(local_cells, rank),
    )(boxes)
    keep, far, sources = spread_boxes(own, peer, groups, total)

    half = rank // 2
    used = rank + SUBLANES + (rank // half + 1) * snapcount
    share = -(-used // (2 * SUBLANES)) * SUBLANES
    sums_shape = like((2 * share, half), F32)
    placed_shape = like((snapcount, local_cells), snaps_box.dtype)
    first = keep.shape[0]
    sums, near, placed = kernel_call(
        lambda *refs: gram_kernel(sources[:first], *refs),
        (sums_shape, like(basis.shape, basis.dtype), placed_shape),
        [VMEM, VMEM, HBM],
        (VMEM, VMEM, VMEM),
        [DMA(())],
        cost_estimate=gram_cost(local_cells, rank),
    )(box_order, keep, basis)
    part = like((share, half), F32)
    mine, send, placed = kernel_call(
        lambda *refs: project_kernel(sources[first:], total, *refs),
        (part, part, placed_shape),
        [VMEM, VMEM, VMEM, VMEM, VMEM],
        (VMEM, VMEM, VMEM),
        [pltpu.VMEM(sums_shape.shape, F32)],
        input_output_aliases={4: 2},
    )(box_order, far, near, sums, placed)

    mine = mine + exchange(send, total, (1, 1))
    masks = flips(total)
    turn = len(masks) // 2
    for pair in zip(masks, masks[turn:] + masks[:turn]):
        mine = mine + exchange(mine, total, pair)
    other = exchange(mine, total, (1, 1))

    modes, coeffs, r_factor, weak = kernel_call(
        lambda *refs: finish_kernel(total, *refs),
        (
            like((snapcount, local_cells), jnp.bfloat16),
            like((snapcount, rank), F32),
            like((snapcount, snapcount), F32),
            like((1, 1), jnp.int32),
        ),
        [VMEM, VMEM, VMEM, VMEM],
        (VMEM, VMEM, VMEM, VMEM),
        [
            pltpu.VMEM(sums_shape.shape, F32),
            pltpu.VMEM((snapcount, local_cells), F32),
        ],
    )(mine, other, placed, near)

    def direct(_):
        residual = placed.astype(F32) - nt(coeffs.astype(jnp.bfloat16), basis)
        wgram = all_sum(jnp.dot(residual, residual.T, precision=HIGH) / cell_total, total)
        lower = jnp.linalg.cholesky(wgram)
        solved = jax.scipy.linalg.solve_triangular(lower, residual, lower=True)
        return solved.astype(jnp.bfloat16), lower.T

    modes, r_factor = _switch_internal(
        weak.reshape(()), (lambda ready: ready, direct), ((modes, r_factor),), branches_platforms=None
    )
    return modes, coeffs, r_factor


def solution(mesh):
    return jax.shard_map(
        local,
        mesh=mesh,
        in_specs=(P(None, AXES), P("rows", None, None), P(AXES, None)),
        out_specs=(P(None, AXES), P(), P()),
        check_vma=False,
    )
```

```python
import jax
import jax.numpy as jnp
from jax import lax
from jax._src.lax.control_flow.conditionals import _switch_internal
from jax.experimental import pallas as pl
from jax.experimental.pallas import tpu as pltpu
from jax.sharding import PartitionSpec as P

AXES = ("rows", "sub")
HIGH = lax.Precision.HIGHEST
LANES, SUBLANES = 128, 8
GUARD = 1.0 / 64.0
STRETCHES = 4
HBM = pl.BlockSpec(memory_space=pltpu.HBM)
ANY = pl.BlockSpec(memory_space=pl.ANY)
DMA = pltpu.SemaphoreType.DMA
LIMIT = 16 * 1048576
VMEM = pl.BlockSpec(memory_space=pltpu.VMEM)
SMEM = pl.BlockSpec(memory_space=pltpu.SMEM)
F32 = jnp.float32


def nt(a, b, precision=None):
    return lax.dot_general(
        a, b, (((1,), (1,)), ((), ())), precision=precision, preferred_element_type=F32
    )


def gram_of(part):
    return lax.dot_general(part, part, (((0,), (0,)), ((), ())), preferred_element_type=F32)


def fetch_kernel(far_ref, near_ref, sem):
    copy = pltpu.make_async_copy(far_ref, near_ref, sem)
    copy.start()
    copy.wait()


def triangle(count):
    shape = (count, count)
    return (
        lax.broadcasted_iota(jnp.int32, shape, 0),
        lax.broadcasted_iota(jnp.int32, shape, 1),
    )


def place_of(order_ref, source):
    position = lax.axis_index("sub")
    order = order_ref[0].astype(F32)
    rows = lax.broadcasted_iota(jnp.int32, order.shape, 0)
    cols = lax.broadcasted_iota(jnp.int32, order.shape, 1)
    wanted = (rows == position) & (cols == position ^ source)
    return jnp.sum(jnp.where(wanted, order, 0.0)).astype(jnp.int32)


def block_sums(sources, order_ref, blocks_ref, basis_ref, placed_ref):
    _, snapcount, block_len = blocks_ref.shape
    raw = jnp.zeros((snapcount, basis_ref.shape[1]), F32)
    own = jnp.zeros((snapcount, snapcount), F32)
    for index, source in enumerate(sources):
        block = blocks_ref[index]
        own += nt(block, block)
        start = pl.multiple_of(place_of(order_ref, source) * block_len, block_len)
        raw += jnp.dot(block, basis_ref[pl.ds(start, block_len), :], preferred_element_type=F32)
        placed_ref[:, pl.ds(start, block_len)] = block
    return raw, own


def gram_kernel(
    sources, order_ref, keep_ref, basis_ref, sums_ref, near_ref, placed_ref, sem
):
    move = pltpu.make_async_copy(basis_ref, near_ref, sem)
    move.start()
    move.wait()
    snapcount = keep_ref.shape[1]
    rank = near_ref.shape[1]
    half = rank // 2
    raw, own = block_sums(sources, order_ref, keep_ref, near_ref, placed_ref)
    total = gram_of(near_ref[...])
    row_id, col_id = triangle(half)
    corner = total[half:, half:]
    sums_ref[0:half] = jnp.where(row_id == col_id, 1.0, 2.0) * jnp.where(
        row_id >= col_id, total[0:half, 0:half], corner
    )
    sums_ref[half:rank] = 2.0 * total[0:half, half:]
    edge = jnp.sum(jnp.where(row_id == col_id, corner, 0.0), axis=0, keepdims=True)
    at = rank
    sums_ref[at : at + SUBLANES] = jnp.broadcast_to(edge, (SUBLANES, half))
    at += SUBLANES
    for part in range(rank // half):
        sums_ref[at : at + snapcount] = raw[:, part * half : (part + 1) * half]
        at += snapcount
    sums_ref[at:] = jnp.zeros((sums_ref.shape[0] - at, half), F32)
    sums_ref[at : at + snapcount, 0:snapcount] = own


def device_index():
    return lax.axis_index("rows") * lax.axis_size("sub") + lax.axis_index("sub")


def parity(device, total):
    value = device
    for bit in range(1, (total - 1).bit_length()):
        value = value ^ (device >> bit)
    return value & 1


def pack_kernel(kept, own_ref, peer_ref, keep_ref, send_ref):
    position = lax.axis_index("sub")
    half = len(kept) // 2
    for source, ref in enumerate((own_ref, peer_ref)):
        for index, offset in enumerate(kept):
            out = keep_ref if index < half else send_ref
            out[source, index % half] = ref[position ^ offset]


def project_kernel(
    sources,
    total,
    order_ref,
    far_ref,
    basis_ref,
    sums_ref,
    placed_in,
    mine_ref,
    send_ref,
    placed_ref,
    out_ref,
):
    snapcount = far_ref.shape[1]
    rank = basis_ref.shape[1]
    half = rank // 2
    share = mine_ref.shape[0]
    placed_ref[...] = placed_in[...]
    raw, own = block_sums(sources, order_ref, far_ref, basis_ref, placed_ref)
    out_ref[...] = sums_ref[...]
    at = rank + SUBLANES
    for part in range(rank // half):
        out_ref[at : at + snapcount] += raw[:, part * half : (part + 1) * half]
        at += snapcount
    out_ref[at : at + snapcount, 0:snapcount] += own
    side = parity(device_index(), total)
    mine_ref[...] = out_ref[pl.ds(pl.multiple_of(side * share, SUBLANES), share)]
    send_ref[...] = out_ref[pl.ds(pl.multiple_of((1 - side) * share, SUBLANES), share)]


def exact_dot(narrow, wide):
    total = None
    for _ in range(3):
        part = wide.astype(jnp.bfloat16)
        wide = wide - part.astype(F32)
        term = jnp.dot(narrow, part, preferred_element_type=F32)
        total = term if total is None else total + term
    return total


def left_exact_nt(wide, narrow):
    parts = []
    for _ in range(3):
        parts.append(wide.astype(jnp.bfloat16))
        wide = wide - parts[-1].astype(F32)
    stacked = nt(jnp.concatenate(parts, axis=0), narrow)
    count = wide.shape[0]
    return stacked[0:count] + stacked[count : 2 * count] + stacked[2 * count :]


def column(matrix, index):
    return matrix[:, index : index + 1]


def factor(gram, scale):
    count = gram.shape[0]
    shape = (count, LANES)
    rows = lax.broadcasted_iota(jnp.int32, shape, 0)
    lanes = lax.broadcasted_iota(jnp.int32, shape, 1)
    columns = [jnp.broadcast_to(column(gram, index), shape) for index in range(count)]
    inverse = [(rows == index).astype(F32) for index in range(count)]
    for step in range(count - 1):
        ratio = columns[step] * (1.0 / columns[step][step : step + 1])
        ratio = jnp.where(rows > step, ratio, 0.0)
        for index in range(step + 1, count):
            columns[index] -= ratio * columns[index][step : step + 1]
        for index in range(step + 1):
            inverse[index] -= ratio * inverse[index][step : step + 1]
    pivots = jnp.zeros(shape, F32)
    upper = jnp.zeros(shape, F32)
    for index in range(count):
        pivots = jnp.where(rows == index, columns[index], pivots)
        upper = jnp.where((lanes == index) & (rows <= index), columns[index], upper)
    sound = pivots[:, 0:1] >= GUARD * scale
    weak = jnp.sum(jnp.where(sound, 0.0, 1.0), axis=0, keepdims=True)
    root = 1.0 / jnp.sqrt(pivots)
    return (upper * root)[:, 0:count], [part * root for part in inverse], weak


def finish_kernel(
    total,
    mine_ref,
    other_ref,
    placed_ref,
    basis_ref,
    modes_ref,
    coeffs_ref,
    upper_ref,
    weak_ref,
    sums_ref,
    resid_ref,
):
    snapcount, cells = placed_ref.shape
    rank = basis_ref.shape[1]
    cell_total = cells * total
    half = rank // 2
    share = mine_ref.shape[0]
    first = parity(device_index(), total) == 0
    sums_ref[0:share] = jnp.where(first, mine_ref[...], other_ref[...])
    sums_ref[share:] = jnp.where(first, other_ref[...], mine_ref[...])
    at = rank + SUBLANES
    parts = []
    for _ in range(rank // half):
        parts.append(sums_ref[at : at + snapcount])
        at += snapcount
    raw = jnp.concatenate(parts, axis=1)
    own = sums_ref[at : at + snapcount, 0:snapcount]
    coeffs = raw / cell_total
    coeffs_ref[...] = coeffs
    narrow = coeffs.astype(jnp.bfloat16)
    rounded = narrow.astype(F32)

    row_id, col_id = triangle(half)
    square = sums_ref[0:half]
    left = jnp.where(row_id >= col_id, square, 0.0)
    right = jnp.concatenate(
        [sums_ref[half:rank], jnp.where(row_id < col_id, square, 0.0)], axis=0
    )
    edge = sums_ref[rank : rank + 1]
    spread = jnp.concatenate(
        [
            exact_dot(narrow[:, 0:half], left),
            exact_dot(narrow, right) + rounded[:, half:] * edge,
        ],
        axis=1,
    )
    pull = left_exact_nt(0.5 * spread - raw, narrow)
    gram = (own + pull + pull.T) / cell_total
    eye = lax.broadcasted_iota(jnp.int32, own.shape, 0) == lax.broadcasted_iota(
        jnp.int32, own.shape, 1
    )
    scale = (
        jnp.sum(jnp.where(eye, own, 0.0), axis=1, keepdims=True)
        + 2.0 * jnp.abs(jnp.sum(raw * rounded, axis=1, keepdims=True))
        + jnp.abs(jnp.sum(spread * rounded, axis=1, keepdims=True))
    ) / cell_total
    upper_factor, columns, weak = factor(gram, scale)
    upper_ref[...] = upper_factor
    weak_ref[...] = (weak > 0.0).astype(jnp.int32)

    stretch = cells // STRETCHES
    for low in range(0, cells, stretch):
        fitted = nt(narrow, basis_ref[low : low + stretch])
        resid_ref[:, low : low + stretch] = (
            placed_ref[:, low : low + stretch].astype(F32) - fitted
        )
    for lane in range(0, cells, LANES):
        modes = columns[0] * resid_ref[0:1, lane : lane + LANES]
        for row in range(1, snapcount):
            modes += columns[row] * resid_ref[row : row + 1, lane : lane + LANES]
        modes_ref[:, lane : lane + LANES] = modes.astype(jnp.bfloat16)


def exchange(value, total, masks):
    def partner(index):
        return index ^ masks[bin(index).count("1") % 2]

    return lax.ppermute(value, AXES, [(index, partner(index)) for index in range(total)])


def flips(count):
    return [(1 << bit) | 1 for bit in range(1, count.bit_length() - 1)]


def all_sum(value, total):
    for mask in [1] + flips(total):
        value = value + exchange(value, total, (mask, mask))
    return value


def kernel_call(kernel, outputs, in_specs, out_specs, scratch=(), **options):
    return pl.pallas_call(
        kernel,
        out_shape=outputs,
        in_specs=in_specs,
        out_specs=out_specs,
        scratch_shapes=scratch,
        compiler_params=pltpu.CompilerParams(vmem_limit_bytes=LIMIT),
        **options,
    )


def spread_boxes(own, peer, groups, total):
    like = jax.ShapeDtypeStruct
    kept, sources = [0], [0, 1]
    for mask in flips(groups):
        kept = kept + [offset ^ mask for offset in kept]
    half = len(kept) // 2
    shape = like((2, half) + own.shape[1:], own.dtype)
    keep, send = kernel_call(
        lambda *refs: pack_kernel(kept, *refs), (shape, shape), [VMEM, VMEM], (VMEM, VMEM)
    )(own, peer)
    for mask in reversed(flips(groups)):
        far = exchange(send, total, (mask, mask))
        sources = sources + [source ^ mask for source in sources]
        if half == 1:
            return keep[:, 0], far[:, 0], sources
        both = jnp.concatenate([keep, far], axis=0)
        half //= 2
        keep, send = both[:, :half], both[:, half:]


def gram_cost(rows, rank):
    return pl.CostEstimate(
        flops=2 * rows * rank * rank, bytes_accessed=2 * rows * rank, transcendentals=0
    )


def local(snaps_box, box_order, basis):
    like = jax.ShapeDtypeStruct
    snapcount = snaps_box.shape[0]
    local_cells, rank = basis.shape
    groups = lax.axis_size("sub")
    total = lax.axis_size("rows") * groups
    block_len = local_cells // groups
    cell_total = local_cells * total

    boxes = snaps_box.reshape(snapcount, groups, block_len).transpose(1, 0, 2)
    peer = exchange(boxes, total, (1, 1))
    own = kernel_call(
        fetch_kernel,
        like(boxes.shape, boxes.dtype),
        [HBM],
        VMEM,
        [DMA(())],
        cost_estimate=gram_cost(local_cells, rank),
    )(boxes)
    keep, far, sources = spread_boxes(own, peer, groups, total)

    half = rank // 2
    used = rank + SUBLANES + (rank // half + 1) * snapcount
    share = -(-used // (2 * SUBLANES)) * SUBLANES
    sums_shape = like((2 * share, half), F32)
    placed_shape = like((snapcount, local_cells), snaps_box.dtype)
    first = keep.shape[0]
    sums, near, placed = kernel_call(
        lambda *refs: gram_kernel(sources[:first], *refs),
        (sums_shape, like(basis.shape, basis.dtype), placed_shape),
        [VMEM, VMEM, HBM],
        (VMEM, VMEM, VMEM),
        [DMA(())],
        cost_estimate=gram_cost(local_cells, rank),
    )(box_order, keep, basis)
    part = like((share, half), F32)
    mine, send, placed = kernel_call(
        lambda *refs: project_kernel(sources[first:], total, *refs),
        (part, part, placed_shape),
        [VMEM, VMEM, VMEM, VMEM, VMEM],
        (VMEM, VMEM, VMEM),
        [pltpu.VMEM(sums_shape.shape, F32)],
    )(box_order, far, near, sums, placed)

    mine = mine + exchange(send, total, (1, 1))
    masks = flips(total)
    turn = len(masks) // 2
    for pair in zip(masks, masks[turn:] + masks[:turn]):
        mine = mine + exchange(mine, total, pair)
    other = exchange(mine, total, (1, 1))

    modes, coeffs, r_factor, weak = kernel_call(
        lambda *refs: finish_kernel(total, *refs),
        (
            like((snapcount, local_cells), jnp.bfloat16),
            like((snapcount, rank), F32),
            like((snapcount, snapcount), F32),
            like((1, 1), jnp.int32),
        ),
        [VMEM, VMEM, VMEM, VMEM],
        (VMEM, VMEM, VMEM, VMEM),
        [
            pltpu.VMEM(sums_shape.shape, F32),
            pltpu.VMEM((snapcount, local_cells), F32),
        ],
    )(mine, other, placed, near)

    def direct(_):
        residual = placed.astype(F32) - nt(coeffs.astype(jnp.bfloat16), basis)
        wgram = all_sum(jnp.dot(residual, residual.T, precision=HIGH) / cell_total, total)
        lower = jnp.linalg.cholesky(wgram)
        solved = jax.scipy.linalg.solve_triangular(lower, residual, lower=True)
        return solved.astype(jnp.bfloat16), lower.T

    modes, r_factor = _switch_internal(
        weak.reshape(()), (lambda ready: ready, direct), ((modes, r_factor),), branches_platforms=None
    )
    return modes, coeffs, r_factor


def solution(mesh):
    return jax.shard_map(
        local,
        mesh=mesh,
        in_specs=(P(None, AXES), P("rows", None, None), P(AXES, None)),
        out_specs=(P(None, AXES), P(), P()),
        check_vma=False,
    )
```

```python
import jax
import jax.numpy as jnp
from jax import lax
from jax._src.lax.control_flow.conditionals import _switch_internal
from jax.experimental import pallas as pl
from jax.experimental.pallas import tpu as pltpu
from jax.sharding import PartitionSpec as P

AXES = ("rows", "sub")
HIGH = lax.Precision.HIGHEST
LANES, SUBLANES = 128, 8
GUARD = 1.0 / 64.0
STRETCHES = 4
HBM = pl.BlockSpec(memory_space=pltpu.HBM)
ANY = pl.BlockSpec(memory_space=pl.ANY)
DMA = pltpu.SemaphoreType.DMA
LIMIT = 16 * 1048576
VMEM = pl.BlockSpec(memory_space=pltpu.VMEM)
SMEM = pl.BlockSpec(memory_space=pltpu.SMEM)
F32 = jnp.float32


def nt(a, b, precision=None):
    return lax.dot_general(
        a, b, (((1,), (1,)), ((), ())), precision=precision, preferred_element_type=F32
    )


def gram_of(part):
    return lax.dot_general(part, part, (((0,), (0,)), ((), ())), preferred_element_type=F32)


def fetch_kernel(far_ref, near_ref, sem):
    copy = pltpu.make_async_copy(far_ref, near_ref, sem)
    copy.start()
    copy.wait()


def triangle(count):
    shape = (count, count)
    return (
        lax.broadcasted_iota(jnp.int32, shape, 0),
        lax.broadcasted_iota(jnp.int32, shape, 1),
    )


def place_of(order_ref, source):
    position = lax.axis_index("sub")
    order = order_ref[0].astype(F32)
    rows = lax.broadcasted_iota(jnp.int32, order.shape, 0)
    cols = lax.broadcasted_iota(jnp.int32, order.shape, 1)
    wanted = (rows == position) & (cols == position ^ source)
    return jnp.sum(jnp.where(wanted, order, 0.0)).astype(jnp.int32)


def block_sums(sources, order_ref, blocks_ref, basis_ref, placed_ref):
    _, snapcount, block_len = blocks_ref.shape
    raw = jnp.zeros((snapcount, basis_ref.shape[1]), F32)
    own = jnp.zeros((snapcount, snapcount), F32)
    for index, source in enumerate(sources):
        block = blocks_ref[index]
        own += nt(block, block)
        start = pl.multiple_of(place_of(order_ref, source) * block_len, block_len)
        raw += jnp.dot(block, basis_ref[pl.ds(start, block_len), :], preferred_element_type=F32)
        placed_ref[:, pl.ds(start, block_len)] = block
    return raw, own


def gram_kernel(
    sources, order_ref, keep_ref, basis_ref, sums_ref, near_ref, placed_ref, sem
):
    move = pltpu.make_async_copy(basis_ref, near_ref, sem)
    move.start()
    move.wait()
    snapcount = keep_ref.shape[1]
    rank = near_ref.shape[1]
    half = rank // 2
    raw, own = block_sums(sources, order_ref, keep_ref, near_ref, placed_ref)
    total = gram_of(near_ref[...])
    row_id, col_id = triangle(half)
    corner = total[half:, half:]
    sums_ref[0:half] = jnp.where(row_id == col_id, 1.0, 2.0) * jnp.where(
        row_id >= col_id, total[0:half, 0:half], corner
    )
    sums_ref[half:rank] = 2.0 * total[0:half, half:]
    edge = jnp.sum(jnp.where(row_id == col_id, corner, 0.0), axis=0, keepdims=True)
    at = rank
    sums_ref[at : at + SUBLANES] = jnp.broadcast_to(edge, (SUBLANES, half))
    at += SUBLANES
    for part in range(rank // half):
        sums_ref[at : at + snapcount] = raw[:, part * half : (part + 1) * half]
        at += snapcount
    sums_ref[at:] = jnp.zeros((sums_ref.shape[0] - at, half), F32)
    sums_ref[at : at + snapcount, 0:snapcount] = own


def device_index():
    return lax.axis_index("rows") * lax.axis_size("sub") + lax.axis_index("sub")


def parity(device, total):
    value = device
    for bit in range(1, (total - 1).bit_length()):
        value = value ^ (device >> bit)
    return value & 1


def pack_kernel(kept, own_ref, peer_ref, keep_ref, send_ref):
    position = lax.axis_index("sub")
    half = len(kept) // 2
    for source, ref in enumerate((own_ref, peer_ref)):
        for index, offset in enumerate(kept):
            out = keep_ref if index < half else send_ref
            out[source, index % half] = ref[position ^ offset]


def project_kernel(
    sources,
    total,
    order_ref,
    far_ref,
    basis_ref,
    sums_ref,
    placed_in,
    mine_ref,
    send_ref,
    placed_ref,
):
    snapcount = far_ref.shape[1]
    rank = basis_ref.shape[1]
    half = rank // 2
    share = mine_ref.shape[0]
    placed_ref[...] = placed_in[...]
    raw, own = block_sums(sources, order_ref, far_ref, basis_ref, placed_ref)
    side = parity(device_index(), total)
    mine_ref[...] = sums_ref[pl.ds(pl.multiple_of(side * share, SUBLANES), share)]
    send_ref[...] = sums_ref[pl.ds(pl.multiple_of((1 - side) * share, SUBLANES), share)]
    keeps = side == 1
    at = rank + SUBLANES - share
    for part in range(rank // half):
        term = raw[:, part * half : (part + 1) * half]
        mine_ref[at : at + snapcount] += jnp.where(keeps, term, 0.0)
        send_ref[at : at + snapcount] += jnp.where(keeps, 0.0, term)
        at += snapcount
    mine_ref[at : at + snapcount, 0:snapcount] += jnp.where(keeps, own, 0.0)
    send_ref[at : at + snapcount, 0:snapcount] += jnp.where(keeps, 0.0, own)


def exact_dot(narrow, wide):
    total = None
    for _ in range(3):
        part = wide.astype(jnp.bfloat16)
        wide = wide - part.astype(F32)
        term = jnp.dot(narrow, part, preferred_element_type=F32)
        total = term if total is None else total + term
    return total


def left_exact_nt(wide, narrow):
    parts = []
    for _ in range(3):
        parts.append(wide.astype(jnp.bfloat16))
        wide = wide - parts[-1].astype(F32)
    stacked = nt(jnp.concatenate(parts, axis=0), narrow)
    count = wide.shape[0]
    return stacked[0:count] + stacked[count : 2 * count] + stacked[2 * count :]


def column(matrix, index):
    return matrix[:, index : index + 1]


def factor(gram, scale):
    count = gram.shape[0]
    shape = (count, LANES)
    rows = lax.broadcasted_iota(jnp.int32, shape, 0)
    lanes = lax.broadcasted_iota(jnp.int32, shape, 1)
    columns = [jnp.broadcast_to(column(gram, index), shape) for index in range(count)]
    inverse = [(rows == index).astype(F32) for index in range(count)]
    for step in range(count - 1):
        ratio = columns[step] * (1.0 / columns[step][step : step + 1])
        ratio = jnp.where(rows > step, ratio, 0.0)
        for index in range(step + 1, count):
            columns[index] -= ratio * columns[index][step : step + 1]
        for index in range(step + 1):
            inverse[index] -= ratio * inverse[index][step : step + 1]
    pivots = jnp.zeros(shape, F32)
    upper = jnp.zeros(shape, F32)
    for index in range(count):
        pivots = jnp.where(rows == index, columns[index], pivots)
        upper = jnp.where((lanes == index) & (rows <= index), columns[index], upper)
    sound = pivots[:, 0:1] >= GUARD * scale
    weak = jnp.sum(jnp.where(sound, 0.0, 1.0), axis=0, keepdims=True)
    root = 1.0 / jnp.sqrt(pivots)
    return (upper * root)[:, 0:count], [part * root for part in inverse], weak


def finish_kernel(
    total,
    mine_ref,
    other_ref,
    placed_ref,
    basis_ref,
    modes_ref,
    coeffs_ref,
    upper_ref,
    weak_ref,
    sums_ref,
    resid_ref,
):
    snapcount, cells = placed_ref.shape
    rank = basis_ref.shape[1]
    cell_total = cells * total
    half = rank // 2
    share = mine_ref.shape[0]
    first = parity(device_index(), total) == 0
    sums_ref[0:share] = jnp.where(first, mine_ref[...], other_ref[...])
    sums_ref[share:] = jnp.where(first, other_ref[...], mine_ref[...])
    at = rank + SUBLANES
    parts = []
    for _ in range(rank // half):
        parts.append(sums_ref[at : at + snapcount])
        at += snapcount
    raw = jnp.concatenate(parts, axis=1)
    own = sums_ref[at : at + snapcount, 0:snapcount]
    coeffs = raw / cell_total
    coeffs_ref[...] = coeffs
    narrow = coeffs.astype(jnp.bfloat16)
    rounded = narrow.astype(F32)

    row_id, col_id = triangle(half)
    square = sums_ref[0:half]
    left = jnp.where(row_id >= col_id, square, 0.0)
    right = jnp.concatenate(
        [sums_ref[half:rank], jnp.where(row_id < col_id, square, 0.0)], axis=0
    )
    edge = sums_ref[rank : rank + 1]
    spread = jnp.concatenate(
        [
            exact_dot(narrow[:, 0:half], left),
            exact_dot(narrow, right) + rounded[:, half:] * edge,
        ],
        axis=1,
    )
    pull = left_exact_nt(0.5 * spread - raw, narrow)
    gram = (own + pull + pull.T) / cell_total
    eye = lax.broadcasted_iota(jnp.int32, own.shape, 0) == lax.broadcasted_iota(
        jnp.int32, own.shape, 1
    )
    scale = (
        jnp.sum(jnp.where(eye, own, 0.0), axis=1, keepdims=True)
        + 2.0 * jnp.abs(jnp.sum(raw * rounded, axis=1, keepdims=True))
        + jnp.abs(jnp.sum(spread * rounded, axis=1, keepdims=True))
    ) / cell_total
    upper_factor, columns, weak = factor(gram, scale)
    upper_ref[...] = upper_factor
    weak_ref[...] = (weak > 0.0).astype(jnp.int32)

    stretch = cells // STRETCHES
    for low in range(0, cells, stretch):
        fitted = nt(narrow, basis_ref[low : low + stretch])
        resid_ref[:, low : low + stretch] = (
            placed_ref[:, low : low + stretch].astype(F32) - fitted
        )
    for lane in range(0, cells, LANES):
        modes = columns[0] * resid_ref[0:1, lane : lane + LANES]
        for row in range(1, snapcount):
            modes += columns[row] * resid_ref[row : row + 1, lane : lane + LANES]
        modes_ref[:, lane : lane + LANES] = modes.astype(jnp.bfloat16)


def exchange(value, total, masks):
    def partner(index):
        return index ^ masks[bin(index).count("1") % 2]

    return lax.ppermute(value, AXES, [(index, partner(index)) for index in range(total)])


def flips(count):
    return [(1 << bit) | 1 for bit in range(1, count.bit_length() - 1)]


def all_sum(value, total):
    for mask in [1] + flips(total):
        value = value + exchange(value, total, (mask, mask))
    return value


def kernel_call(kernel, outputs, in_specs, out_specs, scratch=(), **options):
    return pl.pallas_call(
        kernel,
        out_shape=outputs,
        in_specs=in_specs,
        out_specs=out_specs,
        scratch_shapes=scratch,
        compiler_params=pltpu.CompilerParams(vmem_limit_bytes=LIMIT),
        **options,
    )


def spread_boxes(own, peer, groups, total):
    like = jax.ShapeDtypeStruct
    kept, sources = [0], [0, 1]
    for mask in flips(groups):
        kept = kept + [offset ^ mask for offset in kept]
    half = len(kept) // 2
    shape = like((2, half) + own.shape[1:], own.dtype)
    keep, send = kernel_call(
        lambda *refs: pack_kernel(kept, *refs), (shape, shape), [VMEM, VMEM], (VMEM, VMEM)
    )(own, peer)
    for mask in reversed(flips(groups)):
        far = exchange(send, total, (mask, mask))
        sources = sources + [source ^ mask for source in sources]
        if half == 1:
            return keep[:, 0], far[:, 0], sources
        both = jnp.concatenate([keep, far], axis=0)
        half //= 2
        keep, send = both[:, :half], both[:, half:]


def gram_cost(rows, rank):
    return pl.CostEstimate(
        flops=2 * rows * rank * rank, bytes_accessed=2 * rows * rank, transcendentals=0
    )


def local(snaps_box, box_order, basis):
    like = jax.ShapeDtypeStruct
    snapcount = snaps_box.shape[0]
    local_cells, rank = basis.shape
    groups = lax.axis_size("sub")
    total = lax.axis_size("rows") * groups
    block_len = local_cells // groups
    cell_total = local_cells * total

    boxes = snaps_box.reshape(snapcount, groups, block_len).transpose(1, 0, 2)
    peer = exchange(boxes, total, (1, 1))
    own = kernel_call(
        fetch_kernel,
        like(boxes.shape, boxes.dtype),
        [HBM],
        VMEM,
        [DMA(())],
        cost_estimate=gram_cost(local_cells, rank),
    )(boxes)
    keep, far, sources = spread_boxes(own, peer, groups, total)

    half = rank // 2
    used = rank + SUBLANES + (rank // half + 1) * snapcount
    share = -(-used // (2 * SUBLANES)) * SUBLANES
    sums_shape = like((2 * share, half), F32)
    placed_shape = like((snapcount, local_cells), snaps_box.dtype)
    first = keep.shape[0]
    sums, near, placed = kernel_call(
        lambda *refs: gram_kernel(sources[:first], *refs),
        (sums_shape, like(basis.shape, basis.dtype), placed_shape),
        [VMEM, VMEM, HBM],
        (VMEM, VMEM, VMEM),
        [DMA(())],
        cost_estimate=gram_cost(local_cells, rank),
    )(box_order, keep, basis)
    part = like((share, half), F32)
    mine, send, placed = kernel_call(
        lambda *refs: project_kernel(sources[first:], total, *refs),
        (part, part, placed_shape),
        [VMEM, VMEM, VMEM, VMEM, VMEM],
        (VMEM, VMEM, VMEM),
    )(box_order, far, near, sums, placed)

    mine = mine + exchange(send, total, (1, 1))
    masks = flips(total)
    turn = len(masks) // 2
    for pair in zip(masks, masks[turn:] + masks[:turn]):
        mine = mine + exchange(mine, total, pair)
    other = exchange(mine, total, (1, 1))

    modes, coeffs, r_factor, weak = kernel_call(
        lambda *refs: finish_kernel(total, *refs),
        (
            like((snapcount, local_cells), jnp.bfloat16),
            like((snapcount, rank), F32),
            like((snapcount, snapcount), F32),
            like((1, 1), jnp.int32),
        ),
        [VMEM, VMEM, VMEM, VMEM],
        (VMEM, VMEM, VMEM, VMEM),
        [
            pltpu.VMEM(sums_shape.shape, F32),
            pltpu.VMEM((snapcount, local_cells), F32),
        ],
    )(mine, other, placed, near)

    def direct(_):
        residual = placed.astype(F32) - nt(coeffs.astype(jnp.bfloat16), basis)
        wgram = all_sum(jnp.dot(residual, residual.T, precision=HIGH) / cell_total, total)
        lower = jnp.linalg.cholesky(wgram)
        solved = jax.scipy.linalg.solve_triangular(lower, residual, lower=True)
        return solved.astype(jnp.bfloat16), lower.T

    modes, r_factor = _switch_internal(
        weak.reshape(()), (lambda ready: ready, direct), ((modes, r_factor),), branches_platforms=None
    )
    return modes, coeffs, r_factor


def solution(mesh):
    return jax.shard_map(
        local,
        mesh=mesh,
        in_specs=(P(None, AXES), P("rows", None, None), P(AXES, None)),
        out_specs=(P(None, AXES), P(), P()),
        check_vma=False,
    )
```
